32 devices in a mesh: gx: 8 (over z, y), gy: 4 (over x, core).
Axes of the slice: x: 2, y: 2, z: 4, core: 2. Of those that a mesh axis runs over, the one named last changes fastest.
Arguments:
- positions: float32 [3, 131072], P(None, ('gx', 'gy')), may hold values from 0 to 128, as said below
- mass: float32 [131072], P(('gx', 'gy')), may hold values from 0.5 to 2
- smoothing: float32 [131072], P(('gx', 'gy')), may hold values from 1.5 to 3
- energy: float32 [131072], P(('gx', 'gy')), may hold values from 0.5 to 4
- destination: int32 [131072, 1], P(('gx', 'gy')), may hold values from 0 to 31, as said below
- pairs: int32 [2, 27648], P(None, ('gx', 'gy')), may hold values from 0 to 63, as said below
- pair_count: int32 [32], P(('gx', 'gy')), may hold values from 432 to 864, as said below
Outputs:
- density: float32 [131072], P(('gx', 'gy'))
- accel: float32 [3, 131072], P(None, ('gx', 'gy'))
The draws below stay inside these ranges and needn't reach their ends.
Inputs may be any that keep to these rules, and one draw needn't show every extreme that they name: `destination`: the 4096 particles of every domain name each domain exactly 128 times. `positions`: each particle lies in the box of its new domain (i, j): first coordinate in [16 i, 16 (i + 1)], second in [16 j, 16 (j + 1)], third in [0, 16]. `pairs`: row 0 holds target tiles below 32, row 1 source tiles below 32 + 4 * 8 (tiles from 32 on are ghost tiles); domain d's list is columns d * 864 to (d + 1) * 864 - 1, and slots from pair_count[d] on are unused. `pair_count`: some domain uses all 864 slots.
All inputs are finite; a program needn't handle non-finite values.
Results may differ from the reference program's by a relative error of at most 0.0005.
Values sent between devices are 32-bit elements; how exact they have to be, the bound alone decides.
A program may use at most 64 MiB of HBM per device.

```python
import math
import jax
import jax.numpy as jnp
from jax import lax

P_DEV = 4096
TILE = 128
GT = 8
BOX = 16
NPART = 131072
CAP = 128
NT = 32
MAXP = 864
DEPTH = 16
N_GX = 8
N_GY = 4
DEVICES = 32


def route_plan(key):
    keys = jax.random.split(jax.random.fold_in(key, 31), DEVICES)
    base = jnp.repeat(jnp.arange(DEVICES, dtype=jnp.int32), CAP)
    return jax.vmap(lambda one: jax.random.permutation(one, base))(keys).astype(jnp.int32)


def draw_destination(key, part):
    return route_plan(key).reshape(-1, 1)


def draw_positions(key, part):
    plan = route_plan(key)
    order = jnp.argsort(plan, axis=1, stable=True).astype(jnp.int32)
    placed = jnp.argsort(order, axis=1, stable=True).astype(jnp.int32)
    source = jnp.arange(DEVICES, dtype=jnp.int32)[:, None]
    column = source * CAP + placed - plan * CAP
    edge = column < GT * TILE
    first = (plan // N_GY).astype(jnp.float32)
    second = (plan % N_GY).astype(jnp.float32)
    spread = jax.random.uniform(jax.random.fold_in(key, 41), (3, DEVICES, P_DEV), jnp.float32)
    coord_x = (first + spread[0]) * BOX
    coord_y = (second + spread[1]) * BOX
    coord_z = spread[2] * DEPTH
    face = jax.random.randint(jax.random.fold_in(key, 42), (DEVICES, P_DEV), 0, 4)
    near = jax.random.uniform(jax.random.fold_in(key, 43), (DEVICES, P_DEV), jnp.float32) * 3.0
    coord_x = jnp.where(edge & (face == 0), first * BOX + near, coord_x)
    coord_x = jnp.where(edge & (face == 1), (first + 1.0) * BOX - near, coord_x)
    coord_y = jnp.where(edge & (face == 2), second * BOX + near, coord_y)
    coord_y = jnp.where(edge & (face == 3), (second + 1.0) * BOX - near, coord_y)
    return jnp.stack([coord_x, coord_y, coord_z]).reshape(3, -1).astype(jnp.float32)


def draw_pairs(key, part):
    total = DEVICES * MAXP
    target = jax.random.randint(jax.random.fold_in(key, 11), (total,), 0, NT)
    source = jax.random.randint(jax.random.fold_in(key, 12), (total,), 0, NT + 4 * GT)
    return jnp.stack([target, source]).astype(jnp.int32)


def draw_pair_count(key, part):
    counts = jax.random.randint(jax.random.fold_in(key, 21), (DEVICES,), MAXP // 2, MAXP + 1)
    fullest = jax.random.randint(jax.random.fold_in(key, 22), (), 0, DEVICES)
    return jnp.where(jnp.arange(DEVICES) == fullest, MAXP, counts).astype(jnp.int32)


def shard_levels(own_key, shape, pieces, low, top_value):
    factor_of = 1.0
    for position, blocks in pieces:
        steps = jax.random.uniform(jax.random.fold_in(jax.random.fold_in(own_key, 6), position), (blocks,), jnp.float32, low / len(pieces), top_value / len(pieces))
        factor_of = factor_of * jnp.repeat(jnp.exp(steps), shape[position] // blocks).reshape((-1,) + (1,) * (len(shape) - 1 - position))
    return factor_of


def setup_inputs(seed: int = 0) -> dict:
    streams_of = jax.random.split(jax.random.key(seed), 8)
    positions = draw_positions(jax.random.fold_in(streams_of[7], 71), 0)
    mass = jnp.clip(jnp.exp(math.log(2.0) - 1.3862944 * jax.random.uniform(streams_of[1], (NPART,), jnp.float32) ** shard_levels(streams_of[1], (NPART,), ((0, 32),), -0.2, 0.2)), 0.5, 2.0)
    smoothing = jnp.clip(1.5 + 1.5 * jax.random.uniform(streams_of[2], (NPART,), jnp.float32) ** shard_levels(streams_of[2], (NPART,), ((0, 32),), -0.2, 0.2), 1.5, 3.0)
    energy = jnp.clip(jnp.exp(math.log(4.0) - 2.0794415 * jax.random.uniform(streams_of[3], (NPART,), jnp.float32) ** shard_levels(streams_of[3], (NPART,), ((0, 32),), -0.2, 0.2)), 0.5, 4.0)
    destination = draw_destination(jax.random.fold_in(streams_of[7], 71), 0)
    pairs = draw_pairs(jax.random.fold_in(streams_of[7], 71), 0)
    pair_count = draw_pair_count(jax.random.fold_in(streams_of[7], 71), 0)
    return {"positions": positions, "mass": mass, "smoothing": smoothing, "energy": energy, "destination": destination, "pairs": pairs, "pair_count": pair_count}


KERNEL_NORM = 21.0 / (2.0 * math.pi)
GAMMA_LESS = 2.0 / 3.0

def neighbour_rows(boundary):
    padded = jnp.pad(boundary, ((0, 0), (1, 1), (1, 1), (0, 0)))
    return jnp.concatenate([padded[:, :-2, 1:-1], padded[:, 2:, 1:-1], padded[:, 1:-1, :-2], padded[:, 1:-1, 2:]], axis=3)

def density_domain(pool, pair_list, count, own_tiles):
    slots = pair_list.shape[1]
    group_size = slots // own_tiles
    tile_rows = pool.shape[2]

    def advance(totals, block):
        start = block * group_size
        target = lax.dynamic_slice_in_dim(pair_list[0], start, group_size)
        source = lax.dynamic_slice_in_dim(pair_list[1], start, group_size)
        active = start + jnp.arange(group_size, dtype=jnp.int32) < count
        nearer = pool[target]
        farther = pool[source]
        dist_sq = jnp.zeros((group_size, tile_rows, tile_rows), jnp.float32)
        for component in range(3):
            offset = nearer[:, component, :, None] - farther[:, component, None, :]
            dist_sq = dist_sq + offset * offset
        radius = nearer[:, 4, :, None]
        ratio = jnp.sqrt(dist_sq) / radius
        falloff = jnp.maximum(1.0 - ratio, 0.0)
        kernel = KERNEL_NORM / (radius * radius * radius) * falloff ** 4 * (1.0 + 4.0 * ratio)
        summed = lax.optimization_barrier(jnp.sum(kernel * farther[:, 3, None, :], axis=2))
        summed = jnp.where(active[:, None], summed, 0.0)
        return (totals.at[target].add(summed), None)
    start_totals = jnp.zeros((own_tiles, tile_rows), jnp.float32)
    totals, unused = lax.scan(advance, start_totals, jnp.arange(slots // group_size, dtype=jnp.int32))
    own = pool[:own_tiles]
    radius = own[:, 4, :]
    self_term = own[:, 3, :] * KERNEL_NORM / (radius * radius * radius)
    return (totals + self_term).reshape(-1)

def accel_domain(pool, press_pool, pair_list, count, own_tiles):
    slots = pair_list.shape[1]
    group_size = slots // own_tiles
    tile_rows = pool.shape[2]

    def advance(totals, block):
        start = block * group_size
        target = lax.dynamic_slice_in_dim(pair_list[0], start, group_size)
        source = lax.dynamic_slice_in_dim(pair_list[1], start, group_size)
        active = start + jnp.arange(group_size, dtype=jnp.int32) < count
        nearer = pool[target]
        farther = pool[source]
        press_own = press_pool[target]
        press_far = press_pool[source]
        dist_sq = jnp.zeros((group_size, tile_rows, tile_rows), jnp.float32)
        for component in range(3):
            offset = nearer[:, component, :, None] - farther[:, component, None, :]
            dist_sq = dist_sq + offset * offset
        mean_radius = 0.5 * (nearer[:, 4, :, None] + farther[:, 4, None, :])
        ratio = jnp.sqrt(dist_sq) / mean_radius
        falloff = jnp.maximum(1.0 - ratio, 0.0)
        slope = -20.0 * KERNEL_NORM * falloff ** 3 / mean_radius ** 5
        coupling = farther[:, 3, None, :] * (press_own[:, :, None] + press_far[:, None, :]) * slope
        summed = lax.optimization_barrier(jnp.sum(coupling, axis=2))
        parts_list = []
        for component in range(3):
            pulled = lax.optimization_barrier(jnp.sum(coupling * farther[:, component, None, :], axis=2))
            parts_list.append(-(nearer[:, component, :] * summed - pulled))
        result = jnp.stack(parts_list, axis=1)
        result = jnp.where(active[:, None, None], result, 0.0)
        return (totals.at[target].add(result), None)
    start_totals = jnp.zeros((own_tiles, 3, tile_rows), jnp.float32)
    totals, unused = lax.scan(advance, start_totals, jnp.arange(slots // group_size, dtype=jnp.int32))
    return jnp.transpose(totals, (1, 0, 2)).reshape(3, -1)

def reference(positions, mass, smoothing, energy, destination, pairs, pair_count):
    domains = N_GX * N_GY
    edge_rows = GT * TILE
    fields = jnp.concatenate([positions, mass[None], smoothing[None], energy[None]], 0).reshape(6, domains, P_DEV)
    ranking = jnp.argsort(destination[:, 0].reshape(domains, P_DEV), axis=1, stable=True).astype(jnp.int32)
    outgoing = jnp.take_along_axis(fields, ranking[None], axis=2).reshape(6, domains, domains, CAP)
    settled = jnp.transpose(outgoing, (0, 2, 1, 3)).reshape(6, domains, P_DEV)
    boundary = settled[:, :, :edge_rows].reshape(6, N_GX, N_GY, edge_rows)
    extra = neighbour_rows(boundary).reshape(6, domains, 4 * edge_rows)
    pool = jnp.concatenate([settled, extra], 2).reshape(6, domains, NT + 4 * GT, TILE)
    pool = jnp.transpose(pool, (1, 2, 0, 3))
    pair_lists = jnp.transpose(pairs.reshape(2, domains, MAXP), (1, 0, 2))
    density = lax.map(lambda items: density_domain(items[0], items[1], items[2], NT), (pool, pair_lists, pair_count))
    press = GAMMA_LESS * settled[5] / density
    press_edge = press[:, :edge_rows].reshape(1, N_GX, N_GY, edge_rows)
    press_extra = neighbour_rows(press_edge).reshape(domains, 4 * edge_rows)
    press_pool = jnp.concatenate([press, press_extra], 1).reshape(domains, NT + 4 * GT, TILE)
    accel = lax.map(lambda items: accel_domain(items[0], items[1], items[2], items[3], NT), (pool, press_pool, pair_lists, pair_count))
    accel = jnp.transpose(accel, (1, 0, 2)).reshape(3, -1)
    return (density.reshape(-1), accel)
```

```python
import functools
import math

import jax
import jax.numpy as jnp
from jax import lax
from jax.experimental import pallas as pl
from jax.experimental.pallas import tpu as pltpu
from jax.sharding import PartitionSpec as P

GT = 8
LANES = 128
FEATS = 32
UNROLL = 4
TINY = 1e-12

KERNEL_NORM = 21.0 / (2.0 * math.pi)
GAMMA_LESS = 2.0 / 3.0


def extended(block, sides, width):
    for axis, dim in sides:
        count = lax.axis_size(axis)
        forward = [(i, i + 1) for i in range(count - 1)]
        backward = [(target, source) for source, target in forward]
        low = lax.ppermute(
            lax.slice_in_dim(block, block.shape[dim] - width, None, axis=dim), axis, forward
        )
        high = lax.ppermute(lax.slice_in_dim(block, 0, width, axis=dim), axis, backward)
        block = jnp.concatenate([low, block, high], axis=dim)
    return block


def neighbour_rows(ghosts):
    return jnp.concatenate(
        [ghosts[..., 0, 1, :], ghosts[..., 2, 1, :], ghosts[..., 1, 0, :], ghosts[..., 1, 2, :]],
        axis=-1,
    )


def three(x):
    one = x.astype(jnp.bfloat16).astype(jnp.float32)
    rest = x - one
    two = rest.astype(jnp.bfloat16).astype(jnp.float32)
    return one, two, (rest - two).astype(jnp.bfloat16).astype(jnp.float32)


def source_terms(x):
    one, two, low = three(x)
    return [one, two, one, two, low, one]


def target_terms(x):
    one, two, low = three(x)
    return [one, one, two, two, one, low]


def put_rows(stage, rows, width, tiles):
    for k, row in enumerate(rows):
        stage[pl.ds(k, tiles, stride=width), :] = row


def middle(pool_ref, own_tiles):
    return [
        0.5 * (jnp.min(pool_ref[k, :own_tiles]) + jnp.max(pool_ref[k, :own_tiles]))
        for k in range(3)
    ]


def source_features(coords, extra, stage, tiles):
    norm = sum(c * c for c in coords)
    ones = jnp.ones_like(norm)
    rows = []
    for c in coords + [norm]:
        rows += source_terms(c)
    rows += [ones, ones, ones] + extra
    rows += [jnp.zeros_like(norm)] * (FEATS - len(rows))
    put_rows(stage, rows, FEATS, tiles)


def target_features(coords, scale, stage, tiles):
    norm = sum(c * c for c in coords)
    rows = []
    for c in coords:
        rows += target_terms(-2.0 * c * scale)
    rows += target_terms(scale)
    rows += list(three(norm * scale))
    rows += [jnp.zeros_like(norm)] * (FEATS - len(rows))
    put_rows(stage, rows, FEATS, tiles)


def slot(pairs_ref, count, k, slots, own_tiles):
    live = k < count
    at = jnp.minimum(k, slots - 1)
    target = jnp.where(live, pairs_ref[0, at], 0)
    source = jnp.where(live, pairs_ref[1, at], 0)
    return target, source, jnp.where(live, target, own_tiles)


def density_kernel(count_ref, pairs_ref, pool_ref, dens_ref, press_ref,
                   stage, near, far, mass_b, totals):
    own_tiles = dens_ref.shape[0]
    tiles = pool_ref.shape[1]
    slots = pairs_ref.shape[1]
    centre = middle(pool_ref, own_tiles)
    coords = [pool_ref[k] - centre[k] for k in range(3)]
    source_features(coords, [pool_ref[3]], stage, tiles)

    def turn(t, carry):
        cols = jnp.transpose(stage[pl.ds(t * FEATS, FEATS), :])
        far[t] = cols.astype(jnp.bfloat16)
        mass_b[t] = jnp.broadcast_to(cols[:, 27:28], (LANES, LANES))
        return carry

    lax.fori_loop(0, tiles, turn, 0)
    radius = pool_ref[4, :own_tiles]
    target_features([c[:own_tiles] for c in coords], 1.0 / (radius * radius), stage, own_tiles)

    def keep(t, carry):
        near[t] = stage[pl.ds(t * FEATS, FEATS), :].astype(jnp.bfloat16)
        return carry

    lax.fori_loop(0, own_tiles, keep, 0)
    totals[...] = jnp.zeros_like(totals)
    count = count_ref[0]

    def advance(block, carry):
        for u in range(UNROLL):
            target, source, dest = slot(pairs_ref, count, block * UNROLL + u, slots, own_tiles)
            sq = jnp.dot(far[source], near[target], preferred_element_type=jnp.float32)
            sq = jnp.maximum(sq, TINY)
            ratio = sq * lax.rsqrt(sq)
            falloff = jnp.maximum(1.0 - ratio, 0.0)
            falloff = falloff * falloff
            term = falloff * falloff * ((ratio + 0.25) * mass_b[source])
            totals[dest] += jnp.sum(term.reshape(LANES // 8, 8, LANES), axis=0)
        return carry

    lax.fori_loop(0, (count + UNROLL - 1) // UNROLL, advance, 0)
    summed = jnp.sum(totals[:own_tiles], axis=1)
    norm = KERNEL_NORM / (radius * radius * radius)
    density = norm * (4.0 * summed + pool_ref[3, :own_tiles])
    dens_ref[...] = density
    press_ref[...] = GAMMA_LESS * pool_ref[5, :own_tiles] / density


def accel_kernel(count_ref, pairs_ref, pool_ref, press_ref, out_ref,
                 stage, near, far, half_b, half_a, left, totals):
    own_tiles = out_ref.shape[1]
    tiles = pool_ref.shape[1]
    slots = pairs_ref.shape[1]
    centre = middle(pool_ref, own_tiles)
    coords = [pool_ref[k] - centre[k] for k in range(3)]
    source_features(coords, [0.5 * pool_ref[4]], stage, tiles)

    def turn(t, carry):
        cols = jnp.transpose(stage[pl.ds(t * FEATS, FEATS), :])
        far[t] = cols.astype(jnp.bfloat16)
        half_b[t] = jnp.broadcast_to(cols[:, 27:28], (LANES, LANES))
        return carry

    lax.fori_loop(0, tiles, turn, 0)
    own = [c[:own_tiles] for c in coords]
    target_features(own, jnp.ones_like(own[0]), stage, own_tiles)

    def keep(t, carry):
        near[t] = stage[pl.ds(t * FEATS, FEATS), :].astype(jnp.bfloat16)
        half_a[t] = jnp.broadcast_to(0.5 * pool_ref[4, pl.ds(t, 1), :], (8, LANES))
        return carry

    lax.fori_loop(0, own_tiles, keep, 0)
    mass = pool_ref[3]
    load = mass * press_ref[...]
    rows = [mass] + [mass * c for c in coords] + [load] + [load * c for c in coords]
    split = [three(row) for row in rows]
    put_rows(stage, [s[0] for s in split] + [s[1] for s in split], 16, tiles)

    def pack(t, carry):
        block = stage[pl.ds(t * 16, 16), :].astype(jnp.bfloat16)
        left[t] = jnp.concatenate([block, block], axis=1)
        return carry

    lax.fori_loop(0, tiles, pack, 0)
    totals[...] = jnp.zeros_like(totals)
    count = count_ref[0]

    def advance(block, carry):
        for u in range(UNROLL):
            target, source, dest = slot(pairs_ref, count, block * UNROLL + u, slots, own_tiles)
            sq = jnp.dot(far[source], near[target], preferred_element_type=jnp.float32)
            sq = jnp.maximum(sq, TINY)
            dist = sq * lax.rsqrt(sq)
            radius = half_b[source].reshape(LANES // 8, 8, LANES) + half_a[target][None]
            radius = radius.reshape(LANES, LANES)
            guess = pl.reciprocal(radius, approx=True)
            inv = guess * (2.0 - radius * guess)
            fall = jnp.maximum(inv - dist * (inv * inv), 0.0)
            wide = fall * inv
            slope = wide * wide * fall
            high = slope.astype(jnp.bfloat16)
            low = (slope - high.astype(jnp.float32)).astype(jnp.bfloat16)
            both = jnp.concatenate([high, low], axis=0)
            totals[dest] += jnp.dot(left[source], both, preferred_element_type=jnp.float32)
        return carry

    lax.fori_loop(0, (count + UNROLL - 1) // UNROLL, advance, 0)

    def finish(t, carry):
        sums = totals[t]
        sums = sums[:8] + sums[8:]
        press = press_ref[pl.ds(t, 1), :]
        mixed = press * sums[:4] + sums[4:]
        for k in range(3):
            x = pool_ref[k, pl.ds(t, 1), :] - centre[k]
            out_ref[k, pl.ds(t, 1), :] = 20.0 * KERNEL_NORM * (x * mixed[0:1] - mixed[k + 1:k + 2])
        return carry

    lax.fori_loop(0, own_tiles, finish, 0)


SMEM = pl.BlockSpec(memory_space=pltpu.SMEM)
VMEM = pl.BlockSpec(memory_space=pltpu.VMEM)


def density_call(count, pairs, pool, own_tiles):
    tiles = pool.shape[1]
    flat = jax.ShapeDtypeStruct((own_tiles, LANES), jnp.float32)
    return pl.pallas_call(
        density_kernel,
        out_shape=(flat, flat),
        in_specs=[SMEM, SMEM, VMEM],
        out_specs=(VMEM, VMEM),
        scratch_shapes=[
            pltpu.VMEM((tiles * FEATS, LANES), jnp.float32),
            pltpu.VMEM((own_tiles, FEATS, LANES), jnp.bfloat16),
            pltpu.VMEM((tiles, LANES, FEATS), jnp.bfloat16),
            pltpu.VMEM((tiles, LANES, LANES), jnp.float32),
            pltpu.VMEM((own_tiles + 1, 8, LANES), jnp.float32),
        ],
        name="density",
    )(count, pairs, pool)


def accel_call(count, pairs, pool, press, own_tiles):
    tiles = pool.shape[1]
    return pl.pallas_call(
        accel_kernel,
        out_shape=jax.ShapeDtypeStruct((3, own_tiles, LANES), jnp.float32),
        in_specs=[SMEM, SMEM, VMEM, VMEM],
        out_specs=VMEM,
        scratch_shapes=[
            pltpu.VMEM((tiles * FEATS, LANES), jnp.float32),
            pltpu.VMEM((own_tiles, FEATS, LANES), jnp.bfloat16),
            pltpu.VMEM((tiles, LANES, FEATS), jnp.bfloat16),
            pltpu.VMEM((tiles, LANES, LANES), jnp.float32),
            pltpu.VMEM((own_tiles, 8, LANES), jnp.float32),
            pltpu.VMEM((tiles, 16, 2 * LANES), jnp.bfloat16),
            pltpu.VMEM((own_tiles + 1, 16, LANES), jnp.float32),
        ],
        name="accel",
    )(count, pairs, pool, press)


def local(positions, mass, smoothing, energy, destination, pairs, pair_count):
    across = lax.axis_size("gx")
    beside = lax.axis_size("gy")
    domains = across * beside
    dev_rows = mass.shape[0]
    slot_count = dev_rows // domains
    own_tiles = dev_rows // LANES
    edge_rows = GT * LANES
    fields = jnp.concatenate([positions, mass[None], smoothing[None], energy[None]], 0)
    ranking = jnp.argsort(destination[:, 0], stable=True)
    outgoing = jnp.transpose(fields[:, ranking].reshape(6, domains, slot_count), (1, 0, 2))
    outgoing = outgoing.reshape(across, beside, 6 * slot_count)
    halfway = lax.all_to_all(outgoing, "gy", split_axis=1, concat_axis=1, tiled=True)
    moved = lax.all_to_all(halfway, "gx", split_axis=0, concat_axis=0, tiled=True)
    settled = jnp.transpose(moved.reshape(domains, 6, slot_count), (1, 0, 2)).reshape(6, dev_rows)
    boundary = settled[:, :edge_rows].reshape(6, 1, 1, edge_rows)
    ghosts = extended(boundary, (("gx", 1), ("gy", 2)), 1)
    extra = neighbour_rows(ghosts)
    pool = jnp.concatenate([settled, extra], 1).reshape(6, own_tiles + 4 * GT, LANES)
    density, press = density_call(pair_count, pairs, pool, own_tiles)
    press_edge = press.reshape(-1)[:edge_rows].reshape(1, 1, edge_rows)
    press_ghosts = extended(press_edge, (("gx", 0), ("gy", 1)), 1)
    press_extra = neighbour_rows(press_ghosts).reshape(4 * GT, LANES)
    press_pool = jnp.concatenate([press, press_extra], 0)
    accel = accel_call(pair_count, pairs, pool, press_pool, own_tiles)
    return (density.reshape(-1), accel.reshape(3, -1))


def solution(mesh):
    placed = (
        P(None, ("gx", "gy")),
        P(("gx", "gy")),
        P(("gx", "gy")),
        P(("gx", "gy")),
        P(("gx", "gy"), None),
        P(None, ("gx", "gy")),
        P(("gx", "gy")),
    )
    return jax.shard_map(
        local,
        mesh=mesh,
        in_specs=placed,
        out_specs=(P(("gx", "gy")), P(None, ("gx", "gy"))),
        check_vma=False,
    )
```

```python
import functools
import math

import jax
import jax.numpy as jnp
from jax import lax
from jax.experimental import pallas as pl
from jax.experimental.pallas import tpu as pltpu
from jax.sharding import PartitionSpec as P

GT = 8
LANES = 128
FEATS = 32
TINY = 1e-12

KERNEL_NORM = 21.0 / (2.0 * math.pi)
GAMMA_LESS = 2.0 / 3.0


def extended(block, sides, width):
    for axis, dim in sides:
        count = lax.axis_size(axis)
        forward = [(i, i + 1) for i in range(count - 1)]
        backward = [(target, source) for source, target in forward]
        low = lax.ppermute(
            lax.slice_in_dim(block, block.shape[dim] - width, None, axis=dim), axis, forward
        )
        high = lax.ppermute(lax.slice_in_dim(block, 0, width, axis=dim), axis, backward)
        block = jnp.concatenate([low, block, high], axis=dim)
    return block


def neighbour_rows(ghosts):
    return jnp.concatenate(
        [ghosts[..., 0, 1, :], ghosts[..., 2, 1, :], ghosts[..., 1, 0, :], ghosts[..., 1, 2, :]],
        axis=-1,
    )


def three(x):
    one = x.astype(jnp.bfloat16).astype(jnp.float32)
    rest = x - one
    two = rest.astype(jnp.bfloat16).astype(jnp.float32)
    return one, two, (rest - two).astype(jnp.bfloat16).astype(jnp.float32)


def source_terms(x):
    one, two, low = three(x)
    return [one, two, one, two, low, one]


def target_terms(x):
    one, two, low = three(x)
    return [one, one, two, two, one, low]


def put_rows(stage, rows, width, tiles):
    for k, row in enumerate(rows):
        stage[pl.ds(k, tiles, stride=width), :] = row


def plan_kernel(count_ref, pairs_ref, sizes_ref, own_ref, ghost_ref, times_ref, own_tiles, tiles):
    step = 16

    def clear(block, carry):
        for u in range(step):
            times_ref[block * step + u] = 0
        return carry

    lax.fori_loop(0, times_ref.shape[0] // step, clear, 0)

    def add(k, carry):
        own, ghost = carry
        source = pairs_ref[1, k]
        key = pairs_ref[0, k] * tiles + source
        seen = times_ref[key]
        times_ref[key] = seen + 1
        own_ref[own] = key
        ghost_ref[ghost] = key
        fresh = (seen == 0).astype(jnp.int32)
        near = (source < own_tiles).astype(jnp.int32)
        return own + fresh * near, ghost + fresh * (1 - near)

    own, ghost = lax.fori_loop(0, count_ref[0], add, (0, 0))
    sizes_ref[0] = own
    sizes_ref[1] = ghost


def one_hot_rows(dest):
    rows = lax.broadcasted_iota(jnp.int32, (LANES, LANES), 0)
    wide = jnp.broadcast_to(dest, (LANES, LANES))
    return jnp.where(wide == rows, 1.0, 0.0).astype(jnp.bfloat16)


def by_last(a, b):
    return lax.dot_general(a, b, (((1,), (1,)), ((), ())), preferred_element_type=jnp.float32)


def sweep(list_ref, size, times_ref, tiles, dump, unroll, body):
    last = list_ref.shape[0] - 1

    def advance(block, carry):
        for u in range(unroll):
            k = block * unroll + u
            live = k < size
            key = jnp.where(live, list_ref[jnp.minimum(k, last)], 0)
            target = key // tiles
            source = key - target * tiles
            weight = times_ref[key].astype(jnp.float32)
            body(target, source, jnp.where(live, target, dump), weight)
        return carry

    lax.fori_loop(0, (size + unroll - 1) // unroll, advance, 0)


def keep_rows(stage, near, tiles, base):
    group = 4

    def keep(block, carry):
        for u in range(group):
            t = block * group + u
            near[t, :, base:base + LANES] = stage[pl.ds(t * FEATS, FEATS), :].astype(jnp.bfloat16)
        return carry

    lax.fori_loop(0, tiles // group, keep, 0)


def target_rows(coords, scale, second, stage, near, tiles):
    norm = sum(c * c for c in coords)
    zero = jnp.zeros_like(norm)
    rows = []
    for c in coords:
        rows += target_terms(-2.0 * c * scale)
    rows += target_terms(scale)
    rows += list(three(norm * scale))
    rows += [zero] * (FEATS - len(rows))
    put_rows(stage, rows, FEATS, tiles)
    keep_rows(stage, near, tiles, 0)
    put_rows(stage, [zero] * (FEATS - len(second)) + second, FEATS, tiles)
    keep_rows(stage, near, tiles, LANES)


def density_kernel(sizes_ref, own_ref, ghost_ref, times_ref, pool_ref,
                   dens_ref, press_ref, far, packed_ref, dest_ref, more_ref,
                   stage, near, totals):
    own_tiles = dens_ref.shape[0]
    tiles = pool_ref.shape[1]
    ghosts = tiles - own_tiles
    own, out_of_reach = [], 0.0
    ghost = []
    reach = jnp.max(pool_ref[4]) + 0.01
    for k in range(3):
        x = pool_ref[k, :own_tiles]
        low, high = jnp.min(x), jnp.max(x)
        centre = 0.5 * (low + high)
        far_x = pool_ref[k, own_tiles:]
        gap = jnp.maximum(jnp.maximum(low - far_x, far_x - high), 0.0)
        out_of_reach = out_of_reach + gap * gap
        own.append(x - centre)
        ghost.append(far_x - centre)
    ghost_mass = pool_ref[3, own_tiles:]
    active = (out_of_reach < reach * reach) & (ghost_mass != 0.0)
    upto = lax.broadcasted_iota(jnp.int32, (LANES, LANES), 0) <= lax.broadcasted_iota(
        jnp.int32, (LANES, LANES), 1)
    upto = jnp.where(upto, 1.0, 0.0).astype(jnp.bfloat16)
    flags = jnp.where(active, 1.0, 0.0).astype(jnp.bfloat16)
    rank = jnp.dot(flags, upto, preferred_element_type=jnp.float32)
    dest = jnp.where(active, rank - 1.0, -1.0).astype(jnp.int32)
    dest_ref[...] = dest
    most = jnp.max(rank)
    more = (most > LANES // 2 + 0.5).astype(jnp.int32)
    more_ref[0] = more
    split = [three(x) for x in ghost + [ghost_mass, pool_ref[4, own_tiles:]]]
    zero = jnp.zeros_like(ghost_mass)
    rows = []
    for term in range(3):
        rows += [s[term] for s in split] + [zero] * 3
    put_rows(stage, rows + [zero] * 8, FEATS, ghosts)

    def squeeze(block, carry):
        for u in range(4):
            g = block * 4 + u
            part = stage[pl.ds(g * FEATS, FEATS), :].astype(jnp.bfloat16)
            moved = by_last(part, one_hot_rows(dest_ref[pl.ds(g, 1), :]))
            totals[g] = moved[:8] + moved[8:16] + moved[16:24]
        return carry

    lax.fori_loop(0, ghosts // 4, squeeze, 0)
    fields = []
    for k, x in enumerate(own + [pool_ref[3, :own_tiles], pool_ref[4, :own_tiles]]):
        packed_ref[k, :own_tiles] = x
        packed_ref[k, own_tiles:] = totals[:ghosts, k, :]
        fields.append(packed_ref[k])
    norm = sum(c * c for c in fields[:3])
    ones = jnp.ones_like(norm)
    rows = []
    for c in fields[:3] + [norm]:
        rows += source_terms(c)
    rows += [ones, ones, ones] + list(three(0.5 * fields[4])) + list(three(fields[3])[:2])
    put_rows(stage, rows, FEATS, tiles)

    def turn(g, carry):
        for v in range(2):
            at = g * 2 + v
            cols = jnp.transpose(stage[pl.ds(at * LANES, LANES), :]).astype(jnp.bfloat16)
            for u in range(LANES // FEATS):
                far[at * (LANES // FEATS) + u] = cols[:, u * FEATS:(u + 1) * FEATS]
        return carry

    lax.fori_loop(0, tiles * FEATS // LANES // 2, turn, 0)
    radius = fields[4][:own_tiles]
    one = jnp.ones_like(radius)
    target_rows(own, 1.0 / (radius * radius), [one, one], stage, near, own_tiles)
    totals[...] = jnp.zeros_like(totals)

    def add(first, height):
        def body(target, source, place, weight):
            both = jnp.dot(far[source, first:first + height], near[target],
                           preferred_element_type=jnp.float32)
            sq = jnp.maximum(both[:, :LANES], TINY)
            ratio = sq * lax.rsqrt(sq)
            falloff = jnp.maximum(1.0 - ratio, 0.0)
            falloff = falloff * falloff
            term = falloff * falloff * ((ratio + 0.25) * both[:, LANES:])
            totals[place] += weight * jnp.sum(term.reshape(height // 8, 8, LANES), axis=0)
        return body

    half = LANES // 2
    sweep(own_ref, sizes_ref[0], times_ref, tiles, own_tiles, 4, add(0, LANES))
    sweep(ghost_ref, sizes_ref[1], times_ref, tiles, own_tiles, 8, add(0, half))

    @pl.when(more > 0)
    def _():
        sweep(ghost_ref, sizes_ref[1], times_ref, tiles, own_tiles, 4, add(half, half))

    summed = jnp.sum(totals[:own_tiles], axis=1)
    norm = KERNEL_NORM / (radius * radius * radius)
    density = norm * (4.0 * summed + pool_ref[3, :own_tiles])
    dens_ref[...] = density
    press_ref[...] = GAMMA_LESS * pool_ref[5, :own_tiles] / density


def accel_kernel(sizes_ref, own_ref, ghost_ref, times_ref, more_ref, far, packed_ref, dest_ref,
                 press_ref, press_far_ref, out_ref, stage, near, press_all, left, left_half, totals):
    own_tiles = out_ref.shape[1]
    tiles = packed_ref.shape[1]
    ghosts = tiles - own_tiles
    half = LANES // 2
    zero = jnp.zeros((ghosts, LANES), jnp.float32)
    put_rows(stage, list(three(press_far_ref[...])) + [zero] * 13, 16, ghosts)

    def squeeze(block, carry):
        for u in range(4):
            g = block * 4 + u
            part = stage[pl.ds(g * 16, 16), :].astype(jnp.bfloat16)
            moved = by_last(part, one_hot_rows(dest_ref[pl.ds(g, 1), :]))
            press_all[pl.ds(own_tiles + g, 1), :] = moved[0:1] + moved[1:2] + moved[2:3]
        return carry

    lax.fori_loop(0, ghosts // 4, squeeze, 0)
    press_all[:own_tiles] = press_ref[...]
    own = [packed_ref[k, :own_tiles] for k in range(3)]
    one = jnp.ones_like(own[0])
    none = jnp.zeros_like(own[0])
    second = list(three(0.5 * packed_ref[4, :own_tiles])) + [one, one, one, none, none]
    target_rows(own, one, second, stage, near, own_tiles)
    mass = packed_ref[3]
    load = mass * press_all[...]
    coords = [packed_ref[k] for k in range(3)]
    rows = [mass] + [mass * c for c in coords] + [load] + [load * c for c in coords]
    split = [three(row) for row in rows]
    put_rows(stage, [s[0] for s in split] + [s[1] for s in split], 16, tiles)

    def pack(block, carry):
        for u in range(4):
            t = block * 4 + u
            part = stage[pl.ds(t * 16, 16), :].astype(jnp.bfloat16)
            left[t] = jnp.concatenate([part, part], axis=1)
        return carry

    def pack_half(block, carry):
        for u in range(4):
            t = block * 4 + u
            part = stage[pl.ds((t + own_tiles) * 16, 16), :].astype(jnp.bfloat16)
            for v in range(2):
                piece = part[:, v * half:(v + 1) * half]
                left_half[v, t] = jnp.concatenate([piece, piece], axis=1)
        return carry

    lax.fori_loop(0, own_tiles // 4, pack, 0)
    lax.fori_loop(0, ghosts // 4, pack_half, 0)
    totals[...] = jnp.zeros_like(totals)

    def add(first, height, lhs):
        def body(target, source, place, weight):
            both = jnp.dot(far[source, first:first + height], near[target],
                           preferred_element_type=jnp.float32)
            sq = jnp.maximum(both[:, :LANES], TINY)
            radius = both[:, LANES:]
            dist = sq * lax.rsqrt(sq)
            guess = pl.reciprocal(radius, approx=True)
            inv = guess * (2.0 - radius * guess)
            fall = inv * jnp.maximum(1.0 - dist * inv, 0.0)
            wide = fall * inv
            slope = wide * wide * fall
            high = slope.astype(jnp.bfloat16)
            low = (slope - high.astype(jnp.float32)).astype(jnp.bfloat16)
            terms = jnp.concatenate([high, low], axis=0)
            totals[place] += weight * jnp.dot(lhs(source), terms, preferred_element_type=jnp.float32)
        return body

    sweep(own_ref, sizes_ref[0], times_ref, tiles, own_tiles, 4, add(0, LANES, lambda s: left[s]))
    sweep(ghost_ref, sizes_ref[1], times_ref, tiles, own_tiles, 8,
          add(0, half, lambda s: left_half[0, jnp.maximum(s - own_tiles, 0)]))

    @pl.when(more_ref[0] > 0)
    def _():
        sweep(ghost_ref, sizes_ref[1], times_ref, tiles, own_tiles, 4,
              add(half, half, lambda s: left_half[1, jnp.maximum(s - own_tiles, 0)]))

    folded = totals[:own_tiles, :8] + totals[:own_tiles, 8:]
    mixed = [press_ref[...] * folded[:, k] + folded[:, k + 4] for k in range(4)]
    for k in range(3):
        out_ref[k] = 20.0 * KERNEL_NORM * (own[k] * mixed[0] - mixed[k + 1])


SMEM = pl.BlockSpec(memory_space=pltpu.SMEM)
VMEM = pl.BlockSpec(memory_space=pltpu.VMEM)


def plan_call(count, pairs, own_tiles, tiles):
    slots = pairs.shape[1]
    shapes = [(2,), (slots,), (slots,), (own_tiles * tiles,)]
    return pl.pallas_call(
        functools.partial(plan_kernel, own_tiles=own_tiles, tiles=tiles),
        out_shape=[jax.ShapeDtypeStruct(shape, jnp.int32) for shape in shapes],
        in_specs=[SMEM, SMEM],
        out_specs=[SMEM] * 4,
        cost_estimate=pl.CostEstimate(flops=10 ** 7, bytes_accessed=10 ** 7, transcendentals=0),
        name="plan",
    )(count, pairs)


def density_call(plan, pool, own_tiles):
    tiles = pool.shape[1]
    flat = jax.ShapeDtypeStruct((own_tiles, LANES), jnp.float32)
    return pl.pallas_call(
        density_kernel,
        out_shape=(
            flat,
            flat,
            jax.ShapeDtypeStruct((tiles, LANES, FEATS), jnp.bfloat16),
            jax.ShapeDtypeStruct((5, tiles, LANES), jnp.float32),
            jax.ShapeDtypeStruct((tiles - own_tiles, LANES), jnp.int32),
            jax.ShapeDtypeStruct((1,), jnp.int32),
        ),
        in_specs=[SMEM] * 4 + [VMEM],
        out_specs=(VMEM, VMEM, VMEM, VMEM, VMEM, SMEM),
        scratch_shapes=[
            pltpu.VMEM((tiles * FEATS, LANES), jnp.float32),
            pltpu.VMEM((own_tiles, FEATS, 2 * LANES), jnp.bfloat16),
            pltpu.VMEM((max(own_tiles, tiles - own_tiles) + 1, 8, LANES), jnp.float32),
        ],
        name="density",
    )(*plan, pool)


def accel_call(plan, more, far, packed, dest, press, press_far):
    own_tiles = press.shape[0]
    tiles = packed.shape[1]
    return pl.pallas_call(
        accel_kernel,
        out_shape=jax.ShapeDtypeStruct((3, own_tiles, LANES), jnp.float32),
        in_specs=[SMEM] * 5 + [VMEM] * 5,
        out_specs=VMEM,
        scratch_shapes=[
            pltpu.VMEM((tiles * FEATS, LANES), jnp.float32),
            pltpu.VMEM((own_tiles, FEATS, 2 * LANES), jnp.bfloat16),
            pltpu.VMEM((tiles, LANES), jnp.float32),
            pltpu.VMEM((own_tiles, 16, 2 * LANES), jnp.bfloat16),
            pltpu.VMEM((2, tiles - own_tiles, 16, LANES), jnp.bfloat16),
            pltpu.VMEM((own_tiles + 1, 16, LANES), jnp.float32),
        ],
        name="accel",
    )(*plan, more, far, packed, dest, press, press_far)


def local(positions, mass, smoothing, energy, destination, pairs, pair_count):
    across = lax.axis_size("gx")
    beside = lax.axis_size("gy")
    domains = across * beside
    dev_rows = mass.shape[0]
    slot_count = dev_rows // domains
    own_tiles = dev_rows // LANES
    edge_rows = GT * LANES
    plan = plan_call(pair_count, pairs, own_tiles, own_tiles + 4 * GT)
    fields = jnp.concatenate([positions, mass[None], smoothing[None], energy[None]], 0)
    ranking = jnp.argsort(destination[:, 0], stable=True)
    outgoing = jnp.transpose(fields[:, ranking].reshape(6, domains, slot_count), (1, 0, 2))
    outgoing = outgoing.reshape(across, beside, 6 * slot_count)
    halfway = lax.all_to_all(outgoing, "gy", split_axis=1, concat_axis=1, tiled=True)
    moved = lax.all_to_all(halfway, "gx", split_axis=0, concat_axis=0, tiled=True)
    settled = jnp.transpose(moved.reshape(domains, 6, slot_count), (1, 0, 2)).reshape(6, dev_rows)
    boundary = settled[:, :edge_rows].reshape(6, 1, 1, edge_rows)
    ghosts = extended(boundary, (("gx", 1), ("gy", 2)), 1)
    extra = neighbour_rows(ghosts)
    pool = jnp.concatenate([settled, extra], 1).reshape(6, own_tiles + 4 * GT, LANES)
    density, press, far, packed, dest, more = density_call(plan, pool, own_tiles)
    press_edge = press.reshape(-1)[:edge_rows].reshape(1, 1, edge_rows)
    press_ghosts = extended(press_edge, (("gx", 0), ("gy", 1)), 1)
    press_far = neighbour_rows(press_ghosts).reshape(4 * GT, LANES)
    accel = accel_call(plan, more, far, packed, dest, press, press_far)
    return (density.reshape(-1), accel.reshape(3, -1))


def solution(mesh):
    placed = (
        P(None, ("gx", "gy")),
        P(("gx", "gy")),
        P(("gx", "gy")),
        P(("gx", "gy")),
        P(("gx", "gy"), None),
        P(None, ("gx", "gy")),
        P(("gx", "gy")),
    )
    return jax.shard_map(
        local,
        mesh=mesh,
        in_specs=placed,
        out_specs=(P(("gx", "gy")), P(None, ("gx", "gy"))),
        check_vma=False,
    )
```

```python
import functools
import math

import jax
import jax.numpy as jnp
from jax import lax
from jax.experimental import pallas as pl
from jax.experimental.pallas import tpu as pltpu
from jax.sharding import PartitionSpec as P

GT = 8
LANES = 128
FEATS = 32
TINY = 1e-12

KERNEL_NORM = 21.0 / (2.0 * math.pi)
GAMMA_LESS = 2.0 / 3.0


def extended(block, sides, width):
    for axis, dim in sides:
        count = lax.axis_size(axis)
        forward = [(i, i + 1) for i in range(count - 1)]
        backward = [(target, source) for source, target in forward]
        low = lax.ppermute(
            lax.slice_in_dim(block, block.shape[dim] - width, None, axis=dim), axis, forward
        )
        high = lax.ppermute(lax.slice_in_dim(block, 0, width, axis=dim), axis, backward)
        block = jnp.concatenate([low, block, high], axis=dim)
    return block


def neighbour_rows(ghosts):
    return jnp.concatenate(
        [ghosts[..., 0, 1, :], ghosts[..., 2, 1, :], ghosts[..., 1, 0, :], ghosts[..., 1, 2, :]],
        axis=-1,
    )


def three(x):
    one = x.astype(jnp.bfloat16).astype(jnp.float32)
    rest = x - one
    two = rest.astype(jnp.bfloat16).astype(jnp.float32)
    return one, two, (rest - two).astype(jnp.bfloat16).astype(jnp.float32)


def source_terms(x):
    one, two, low = three(x)
    return [one, two, one, two, low, one]


def target_terms(x):
    one, two, low = three(x)
    return [one, one, two, two, one, low]


def put_rows(stage, rows, width, tiles):
    for k, row in enumerate(rows):
        stage[pl.ds(k, tiles, stride=width), :] = row


def plan_kernel(count_ref, pairs_ref, sizes_ref, own_ref, ghost_ref, times_ref, own_tiles, tiles):
    step = 16

    def clear(block, carry):
        for u in range(step):
            times_ref[block * step + u] = 0
        return carry

    lax.fori_loop(0, times_ref.shape[0] // step, clear, 0)

    count = count_ref[0]
    spare = own_tiles * tiles
    last = pairs_ref.shape[1] - 1
    ahead = 8

    def add(block, carry):
        own, ghost = carry
        picked = []
        for u in range(ahead):
            k = block * ahead + u
            live = k < count
            at = jnp.minimum(k, last)
            source = jnp.where(live, pairs_ref[1, at], 0)
            key = jnp.where(live, pairs_ref[0, at] * tiles + source, spare)
            near = (source < own_tiles).astype(jnp.int32)
            alive = live.astype(jnp.int32)
            picked.append((key, near * alive, (1 - near) * alive))
        for key, near, beyond in picked:
            seen = times_ref[key]
            times_ref[key] = seen + 1
            own_ref[own] = key
            ghost_ref[ghost] = key
            fresh = (seen == 0).astype(jnp.int32)
            own = own + fresh * near
            ghost = ghost + fresh * beyond
        return own, ghost

    own, ghost = lax.fori_loop(0, (count + ahead - 1) // ahead, add, (0, 0))
    sizes_ref[0] = own
    sizes_ref[1] = ghost


def one_hot_rows(dest):
    rows = lax.broadcasted_iota(jnp.int32, (LANES, LANES), 0)
    wide = jnp.broadcast_to(dest, (LANES, LANES))
    return jnp.where(wide == rows, 1.0, 0.0).astype(jnp.bfloat16)


def by_last(a, b):
    return lax.dot_general(a, b, (((1,), (1,)), ((), ())), preferred_element_type=jnp.float32)


def sweep(list_ref, size, times_ref, tiles, dump, unroll, body):
    last = list_ref.shape[0] - 1

    def advance(block, carry):
        for u in range(unroll):
            k = block * unroll + u
            live = k < size
            key = jnp.where(live, list_ref[jnp.minimum(k, last)], 0)
            target = key // tiles
            source = key - target * tiles
            weight = times_ref[key].astype(jnp.float32)
            body(target, source, jnp.where(live, target, dump), weight)
        return carry

    lax.fori_loop(0, (size + unroll - 1) // unroll, advance, 0)


def keep_rows(stage, near, tiles):
    group = 4

    def keep(block, carry):
        for u in range(group):
            t = block * group + u
            near[t] = stage[pl.ds(t * FEATS, FEATS), :].astype(jnp.bfloat16)
        return carry

    lax.fori_loop(0, tiles // group, keep, 0)


def target_rows(coords, scale, stage, near, tiles):
    norm = sum(c * c for c in coords)
    zero = jnp.zeros_like(norm)
    rows = []
    for c in coords:
        rows += target_terms(-2.0 * c * scale)
    rows += target_terms(scale)
    rows += list(three(norm * scale))
    rows += [zero] * (FEATS - len(rows))
    put_rows(stage, rows, FEATS, tiles)
    keep_rows(stage, near, tiles)


def spread_column(far, first, last, wide):
    row = lax.broadcasted_iota(jnp.int32, (FEATS, LANES), 0)
    pick = jnp.where((row >= first) & (row < last), 1.0, 0.0).astype(jnp.bfloat16)
    group = 4

    def one(block, carry):
        for u in range(group):
            t = block * group + u
            wide[t] = jnp.dot(far[t], pick, preferred_element_type=jnp.float32)
        return carry

    lax.fori_loop(0, wide.shape[0] // group, one, 0)


def density_kernel(sizes_ref, own_ref, ghost_ref, times_ref, pool_ref,
                   dens_ref, press_ref, far, packed_ref, dest_ref, more_ref,
                   stage, near, mass_b, totals):
    own_tiles = dens_ref.shape[0]
    tiles = pool_ref.shape[1]
    ghosts = tiles - own_tiles
    own, out_of_reach = [], 0.0
    ghost = []
    reach = jnp.max(pool_ref[4]) + 0.01
    for k in range(3):
        x = pool_ref[k, :own_tiles]
        low, high = jnp.min(x), jnp.max(x)
        centre = 0.5 * (low + high)
        far_x = pool_ref[k, own_tiles:]
        gap = jnp.maximum(jnp.maximum(low - far_x, far_x - high), 0.0)
        out_of_reach = out_of_reach + gap * gap
        own.append(x - centre)
        ghost.append(far_x - centre)
    ghost_mass = pool_ref[3, own_tiles:]
    active = (out_of_reach < reach * reach) & (ghost_mass != 0.0)
    upto = lax.broadcasted_iota(jnp.int32, (LANES, LANES), 0) <= lax.broadcasted_iota(
        jnp.int32, (LANES, LANES), 1)
    upto = jnp.where(upto, 1.0, 0.0).astype(jnp.bfloat16)
    flags = jnp.where(active, 1.0, 0.0).astype(jnp.bfloat16)
    rank = jnp.dot(flags, upto, preferred_element_type=jnp.float32)
    dest = jnp.where(active, rank - 1.0, -1.0).astype(jnp.int32)
    dest_ref[...] = dest
    most = jnp.max(rank)
    more = (most > LANES // 2 + 0.5).astype(jnp.int32)
    more_ref[0] = more
    split = [three(x) for x in ghost + [ghost_mass, pool_ref[4, own_tiles:]]]
    zero = jnp.zeros_like(ghost_mass)
    rows = []
    for term in range(3):
        rows += [s[term] for s in split] + [zero] * 3
    put_rows(stage, rows + [zero] * 8, FEATS, ghosts)

    def squeeze(block, carry):
        for u in range(4):
            g = block * 4 + u
            part = stage[pl.ds(g * FEATS, FEATS), :].astype(jnp.bfloat16)
            moved = by_last(part, one_hot_rows(dest_ref[pl.ds(g, 1), :]))
            totals[g] = moved[:8] + moved[8:16] + moved[16:24]
        return carry

    lax.fori_loop(0, ghosts // 4, squeeze, 0)
    fields = []
    for k, x in enumerate(own + [pool_ref[3, :own_tiles], pool_ref[4, :own_tiles]]):
        packed_ref[k, :own_tiles] = x
        packed_ref[k, own_tiles:] = totals[:ghosts, k, :]
        fields.append(packed_ref[k])
    norm = sum(c * c for c in fields[:3])
    ones = jnp.ones_like(norm)
    rows = []
    for c in fields[:3] + [norm]:
        rows += source_terms(c)
    rows += [ones, ones, ones] + list(three(0.5 * fields[4])) + list(three(fields[3])[:2])
    put_rows(stage, rows, FEATS, tiles)

    def turn(g, carry):
        for v in range(2):
            at = g * 2 + v
            cols = jnp.transpose(stage[pl.ds(at * LANES, LANES), :]).astype(jnp.bfloat16)
            for u in range(LANES // FEATS):
                far[at * (LANES // FEATS) + u] = cols[:, u * FEATS:(u + 1) * FEATS]
        return carry

    lax.fori_loop(0, tiles * FEATS // LANES // 2, turn, 0)
    radius = fields[4][:own_tiles]
    target_rows(own, 1.0 / (radius * radius), stage, near, own_tiles)
    spread_column(far, 30, 32, mass_b)
    totals[...] = jnp.zeros_like(totals)

    def add(first, height):
        def body(target, source, place, weight):
            sq = jnp.dot(far[source, first:first + height], near[target],
                         preferred_element_type=jnp.float32)
            sq = jnp.maximum(sq, TINY)
            ratio = sq * lax.rsqrt(sq)
            falloff = jnp.maximum(1.0 - ratio, 0.0)
            falloff = falloff * falloff
            term = falloff * falloff * ((ratio + 0.25) * mass_b[source, first:first + height])
            totals[place] += weight * jnp.sum(term.reshape(height // 8, 8, LANES), axis=0)
        return body

    half = LANES // 2
    sweep(own_ref, sizes_ref[0], times_ref, tiles, own_tiles, 4, add(0, LANES))
    sweep(ghost_ref, sizes_ref[1], times_ref, tiles, own_tiles, 8, add(0, half))

    @pl.when(more > 0)
    def _():
        sweep(ghost_ref, sizes_ref[1], times_ref, tiles, own_tiles, 4, add(half, half))

    summed = jnp.sum(totals[:own_tiles], axis=1)
    norm = KERNEL_NORM / (radius * radius * radius)
    density = norm * (4.0 * summed + pool_ref[3, :own_tiles])
    dens_ref[...] = density
    press_ref[...] = GAMMA_LESS * pool_ref[5, :own_tiles] / density


def accel_kernel(sizes_ref, own_ref, ghost_ref, times_ref, more_ref, far, packed_ref, dest_ref,
                 press_ref, press_far_ref, out_ref, stage, near, half_a, half_b, press_all, left, left_half,
                 totals):
    own_tiles = out_ref.shape[1]
    tiles = packed_ref.shape[1]
    ghosts = tiles - own_tiles
    half = LANES // 2
    zero = jnp.zeros((ghosts, LANES), jnp.float32)
    put_rows(stage, list(three(press_far_ref[...])) + [zero] * 13, 16, ghosts)

    def squeeze(block, carry):
        for u in range(4):
            g = block * 4 + u
            part = stage[pl.ds(g * 16, 16), :].astype(jnp.bfloat16)
            moved = by_last(part, one_hot_rows(dest_ref[pl.ds(g, 1), :]))
            press_all[pl.ds(own_tiles + g, 1), :] = moved[0:1] + moved[1:2] + moved[2:3]
        return carry

    lax.fori_loop(0, ghosts // 4, squeeze, 0)
    press_all[:own_tiles] = press_ref[...]
    own = [packed_ref[k, :own_tiles] for k in range(3)]
    target_rows(own, jnp.ones_like(own[0]), stage, near, own_tiles)
    spread_column(far, 27, 30, half_b)
    half_a[...] = 0.5 * packed_ref[4, :own_tiles]
    mass = packed_ref[3]
    load = mass * press_all[...]
    coords = [packed_ref[k] for k in range(3)]
    rows = [mass] + [mass * c for c in coords] + [load] + [load * c for c in coords]
    split = [three(row) for row in rows]
    put_rows(stage, [s[0] for s in split] + [s[1] for s in split], 16, tiles)

    def pack(block, carry):
        for u in range(4):
            t = block * 4 + u
            part = stage[pl.ds(t * 16, 16), :].astype(jnp.bfloat16)
            left[t] = jnp.concatenate([part, part], axis=1)
        return carry

    def pack_half(block, carry):
        for u in range(4):
            t = block * 4 + u
            part = stage[pl.ds((t + own_tiles) * 16, 16), :].astype(jnp.bfloat16)
            for v in range(2):
                piece = part[:, v * half:(v + 1) * half]
                left_half[v, t] = jnp.concatenate([piece, piece], axis=1)
        return carry

    lax.fori_loop(0, own_tiles // 4, pack, 0)
    lax.fori_loop(0, ghosts // 4, pack_half, 0)
    totals[...] = jnp.zeros_like(totals)

    def add(first, height, lhs):
        def body(target, source, place, weight):
            sq = jnp.dot(far[source, first:first + height], near[target],
                         preferred_element_type=jnp.float32)
            sq = jnp.maximum(sq, TINY)
            radius = half_b[source, first:first + height] + half_a[pl.ds(target, 1), :]
            dist = sq * lax.rsqrt(sq)
            guess = pl.reciprocal(radius, approx=True)
            inv = guess * (2.0 - radius * guess)
            fall = inv * jnp.maximum(1.0 - dist * inv, 0.0)
            wide = fall * inv
            slope = wide * wide * fall
            high = slope.astype(jnp.bfloat16)
            low = (slope - high.astype(jnp.float32)).astype(jnp.bfloat16)
            terms = jnp.concatenate([high, low], axis=0)
            totals[place] += weight * jnp.dot(lhs(source), terms, preferred_element_type=jnp.float32)
        return body

    sweep(own_ref, sizes_ref[0], times_ref, tiles, own_tiles, 4, add(0, LANES, lambda s: left[s]))
    sweep(ghost_ref, sizes_ref[1], times_ref, tiles, own_tiles, 8,
          add(0, half, lambda s: left_half[0, jnp.maximum(s - own_tiles, 0)]))

    @pl.when(more_ref[0] > 0)
    def _():
        sweep(ghost_ref, sizes_ref[1], times_ref, tiles, own_tiles, 4,
              add(half, half, lambda s: left_half[1, jnp.maximum(s - own_tiles, 0)]))

    folded = totals[:own_tiles, :8] + totals[:own_tiles, 8:]
    mixed = [press_ref[...] * folded[:, k] + folded[:, k + 4] for k in range(4)]
    for k in range(3):
        out_ref[k] = 20.0 * KERNEL_NORM * (own[k] * mixed[0] - mixed[k + 1])


SMEM = pl.BlockSpec(memory_space=pltpu.SMEM)
VMEM = pl.BlockSpec(memory_space=pltpu.VMEM)


def plan_call(count, pairs, own_tiles, tiles):
    slots = pairs.shape[1]
    shapes = [(2,), (slots + 1,), (slots + 1,), (own_tiles * tiles + LANES,)]
    return pl.pallas_call(
        functools.partial(plan_kernel, own_tiles=own_tiles, tiles=tiles),
        out_shape=[jax.ShapeDtypeStruct(shape, jnp.int32) for shape in shapes],
        in_specs=[SMEM, SMEM],
        out_specs=[SMEM] * 4,
        cost_estimate=pl.CostEstimate(flops=10 ** 7, bytes_accessed=10 ** 7, transcendentals=0),
        name="plan",
    )(count, pairs)


def density_call(plan, pool, own_tiles):
    tiles = pool.shape[1]
    flat = jax.ShapeDtypeStruct((own_tiles, LANES), jnp.float32)
    return pl.pallas_call(
        density_kernel,
        out_shape=(
            flat,
            flat,
            jax.ShapeDtypeStruct((tiles, LANES, FEATS), jnp.bfloat16),
            jax.ShapeDtypeStruct((5, tiles, LANES), jnp.float32),
            jax.ShapeDtypeStruct((tiles - own_tiles, LANES), jnp.int32),
            jax.ShapeDtypeStruct((1,), jnp.int32),
        ),
        in_specs=[SMEM] * 4 + [VMEM],
        out_specs=(VMEM, VMEM, VMEM, VMEM, VMEM, SMEM),
        scratch_shapes=[
            pltpu.VMEM((tiles * FEATS, LANES), jnp.float32),
            pltpu.VMEM((own_tiles, FEATS, LANES), jnp.bfloat16),
            pltpu.VMEM((tiles, LANES, LANES), jnp.float32),
            pltpu.VMEM((max(own_tiles, tiles - own_tiles) + 1, 8, LANES), jnp.float32),
        ],
        name="density",
    )(*plan, pool)


def accel_call(plan, more, far, packed, dest, press, press_far):
    own_tiles = press.shape[0]
    tiles = packed.shape[1]
    return pl.pallas_call(
        accel_kernel,
        out_shape=jax.ShapeDtypeStruct((3, own_tiles, LANES), jnp.float32),
        in_specs=[SMEM] * 5 + [VMEM] * 5,
        out_specs=VMEM,
        scratch_shapes=[
            pltpu.VMEM((tiles * FEATS, LANES), jnp.float32),
            pltpu.VMEM((own_tiles, FEATS, LANES), jnp.bfloat16),
            pltpu.VMEM((own_tiles, LANES), jnp.float32),
            pltpu.VMEM((tiles, LANES, LANES), jnp.float32),
            pltpu.VMEM((tiles, LANES), jnp.float32),
            pltpu.VMEM((own_tiles, 16, 2 * LANES), jnp.bfloat16),
            pltpu.VMEM((2, tiles - own_tiles, 16, LANES), jnp.bfloat16),
            pltpu.VMEM((own_tiles + 1, 16, LANES), jnp.float32),
        ],
        name="accel",
    )(*plan, more, far, packed, dest, press, press_far)


def local(positions, mass, smoothing, energy, destination, pairs, pair_count):
    across = lax.axis_size("gx")
    beside = lax.axis_size("gy")
    domains = across * beside
    dev_rows = mass.shape[0]
    slot_count = dev_rows // domains
    own_tiles = dev_rows // LANES
    edge_rows = GT * LANES
    plan = plan_call(pair_count, pairs, own_tiles, own_tiles + 4 * GT)
    fields = jnp.concatenate([positions, mass[None], smoothing[None], energy[None]], 0)
    ordered = lax.sort(
        (destination[:, 0],) + tuple(fields[k] for k in range(6)), num_keys=1, is_stable=True
    )
    outgoing = jnp.stack([row.reshape(domains, slot_count) for row in ordered[1:]], 1)
    outgoing = outgoing.reshape(across, beside, 6 * slot_count)
    halfway = lax.all_to_all(outgoing, "gy", split_axis=1, concat_axis=1, tiled=True)
    moved = lax.all_to_all(halfway, "gx", split_axis=0, concat_axis=0, tiled=True)
    settled = jnp.transpose(moved.reshape(domains, 6, slot_count), (1, 0, 2)).reshape(6, dev_rows)
    boundary = settled[:, :edge_rows].reshape(6, 1, 1, edge_rows)
    ghosts = extended(boundary, (("gx", 1), ("gy", 2)), 1)
    extra = neighbour_rows(ghosts)
    pool = jnp.concatenate([settled, extra], 1).reshape(6, own_tiles + 4 * GT, LANES)
    density, press, far, packed, dest, more = density_call(plan, pool, own_tiles)
    press_edge = press.reshape(-1)[:edge_rows].reshape(1, 1, edge_rows)
    press_ghosts = extended(press_edge, (("gx", 0), ("gy", 1)), 1)
    press_far = neighbour_rows(press_ghosts).reshape(4 * GT, LANES)
    accel = accel_call(plan, more, far, packed, dest, press, press_far)
    return (density.reshape(-1), accel.reshape(3, -1))


def solution(mesh):
    placed = (
        P(None, ("gx", "gy")),
        P(("gx", "gy")),
        P(("gx", "gy")),
        P(("gx", "gy")),
        P(("gx", "gy"), None),
        P(None, ("gx", "gy")),
        P(("gx", "gy")),
    )
    return jax.shard_map(
        local,
        mesh=mesh,
        in_specs=placed,
        out_specs=(P(("gx", "gy")), P(None, ("gx", "gy"))),
        check_vma=False,
    )
```

```python
import functools
import math

import jax
import jax.numpy as jnp
from jax import lax
from jax.experimental import pallas as pl
from jax.experimental.pallas import tpu as pltpu
from jax.sharding import PartitionSpec as P

GT = 8
LANES = 128
FEATS = 32
TINY = 1e-12

KERNEL_NORM = 21.0 / (2.0 * math.pi)
GAMMA_LESS = 2.0 / 3.0


def extended(block, sides, width):
    for axis, dim in sides:
        count = lax.axis_size(axis)
        forward = [(i, i + 1) for i in range(count - 1)]
        backward = [(target, source) for source, target in forward]
        low = lax.ppermute(
            lax.slice_in_dim(block, block.shape[dim] - width, None, axis=dim), axis, forward
        )
        high = lax.ppermute(lax.slice_in_dim(block, 0, width, axis=dim), axis, backward)
        block = jnp.concatenate([low, block, high], axis=dim)
    return block


def neighbour_rows(ghosts):
    return jnp.concatenate(
        [ghosts[..., 0, 1, :], ghosts[..., 2, 1, :], ghosts[..., 1, 0, :], ghosts[..., 1, 2, :]],
        axis=-1,
    )


def three(x):
    one = x.astype(jnp.bfloat16).astype(jnp.float32)
    rest = x - one
    two = rest.astype(jnp.bfloat16).astype(jnp.float32)
    return one, two, (rest - two).astype(jnp.bfloat16).astype(jnp.float32)


def source_terms(x):
    one, two, low = three(x)
    return [one, two, one, two, low, one]


def target_terms(x):
    one, two, low = three(x)
    return [one, one, two, two, one, low]


def put_rows(stage, rows, width, tiles):
    for k, row in enumerate(rows):
        stage[pl.ds(k, tiles, stride=width), :] = row


def plan_kernel(count_ref, pairs_ref, sizes_ref, own_ref, ghost_ref, times_ref, own_tiles, tiles):
    step = 16

    def clear(block, carry):
        for u in range(step):
            times_ref[block * step + u] = 0
        return carry

    lax.fori_loop(0, times_ref.shape[0] // step, clear, 0)

    count = count_ref[0]
    spare = own_tiles * tiles
    last = pairs_ref.shape[1] - 1
    ahead = 8

    def add(block, carry):
        own, ghost = carry
        picked = []
        for u in range(ahead):
            k = block * ahead + u
            live = k < count
            at = jnp.minimum(k, last)
            source = jnp.where(live, pairs_ref[1, at], 0)
            key = jnp.where(live, pairs_ref[0, at] * tiles + source, spare)
            near = (source < own_tiles).astype(jnp.int32)
            alive = live.astype(jnp.int32)
            picked.append((key, near * alive, (1 - near) * alive))
        for key, near, beyond in picked:
            seen = times_ref[key]
            times_ref[key] = seen + 1
            own_ref[own] = key
            ghost_ref[ghost] = key
            fresh = (seen == 0).astype(jnp.int32)
            own = own + fresh * near
            ghost = ghost + fresh * beyond
        return own, ghost

    own, ghost = lax.fori_loop(0, (count + ahead - 1) // ahead, add, (0, 0))
    sizes_ref[0] = own
    sizes_ref[1] = ghost


def one_hot_rows(dest):
    rows = lax.broadcasted_iota(jnp.int32, (LANES, LANES), 0)
    wide = jnp.broadcast_to(dest, (LANES, LANES))
    return jnp.where(wide == rows, 1.0, 0.0).astype(jnp.bfloat16)


def by_last(a, b):
    return lax.dot_general(a, b, (((1,), (1,)), ((), ())), preferred_element_type=jnp.float32)


def sweep(list_ref, size, times_ref, tiles, dump, unroll, body):
    last = list_ref.shape[0] - 1

    def advance(block, carry):
        for u in range(unroll):
            k = block * unroll + u
            live = k < size
            key = jnp.where(live, list_ref[jnp.minimum(k, last)], 0)
            target = key // tiles
            source = key - target * tiles
            weight = times_ref[key].astype(jnp.float32)
            body(target, source, jnp.where(live, target, dump), weight)
        return carry

    lax.fori_loop(0, (size + unroll - 1) // unroll, advance, 0)


def keep_rows(stage, near, tiles):
    group = 4

    def keep(block, carry):
        for u in range(group):
            t = block * group + u
            near[t] = stage[pl.ds(t * FEATS, FEATS), :].astype(jnp.bfloat16)
        return carry

    lax.fori_loop(0, tiles // group, keep, 0)


def target_rows(coords, scale, stage, near, tiles):
    norm = sum(c * c for c in coords)
    zero = jnp.zeros_like(norm)
    rows = []
    for c in coords:
        rows += target_terms(-2.0 * c * scale)
    rows += target_terms(scale)
    rows += list(three(norm * scale))
    rows += [zero] * (FEATS - len(rows))
    put_rows(stage, rows, FEATS, tiles)
    keep_rows(stage, near, tiles)


def spread_column(far, first, last, wide):
    row = lax.broadcasted_iota(jnp.int32, (FEATS, LANES), 0)
    pick = jnp.where((row >= first) & (row < last), 1.0, 0.0).astype(jnp.bfloat16)
    group = 4

    def one(block, carry):
        for u in range(group):
            t = block * group + u
            wide[t] = jnp.dot(far[t], pick, preferred_element_type=jnp.float32)
        return carry

    lax.fori_loop(0, wide.shape[0] // group, one, 0)


def density_kernel(sizes_ref, own_ref, ghost_ref, times_ref, pool_ref,
                   dens_ref, press_ref, far, packed_ref, dest_ref, more_ref,
                   stage, near, mass_b, totals):
    own_tiles = dens_ref.shape[0]
    tiles = pool_ref.shape[1]
    ghosts = tiles - own_tiles
    own, out_of_reach = [], 0.0
    ghost = []
    reach = jnp.max(pool_ref[4]) + 0.01
    for k in range(3):
        x = pool_ref[k, :own_tiles]
        low, high = jnp.min(x), jnp.max(x)
        centre = 0.5 * (low + high)
        far_x = pool_ref[k, own_tiles:]
        gap = jnp.maximum(jnp.maximum(low - far_x, far_x - high), 0.0)
        out_of_reach = out_of_reach + gap * gap
        own.append(x - centre)
        ghost.append(far_x - centre)
    ghost_mass = pool_ref[3, own_tiles:]
    active = (out_of_reach < reach * reach) & (ghost_mass != 0.0)
    upto = lax.broadcasted_iota(jnp.int32, (LANES, LANES), 0) <= lax.broadcasted_iota(
        jnp.int32, (LANES, LANES), 1)
    upto = jnp.where(upto, 1.0, 0.0).astype(jnp.bfloat16)
    flags = jnp.where(active, 1.0, 0.0).astype(jnp.bfloat16)
    rank = jnp.dot(flags, upto, preferred_element_type=jnp.float32)
    dest = jnp.where(active, rank - 1.0, -1.0).astype(jnp.int32)
    dest_ref[...] = dest
    most = jnp.max(rank)
    more = (most > LANES // 2 + 0.5).astype(jnp.int32)
    more_ref[0] = more
    split = [three(x) for x in ghost + [ghost_mass, pool_ref[4, own_tiles:]]]
    zero = jnp.zeros_like(ghost_mass)
    rows = []
    for term in range(3):
        rows += [s[term] for s in split] + [zero] * 3
    put_rows(stage, rows + [zero] * 8, FEATS, ghosts)

    def squeeze(block, carry):
        for u in range(4):
            g = block * 4 + u
            part = stage[pl.ds(g * FEATS, FEATS), :].astype(jnp.bfloat16)
            moved = by_last(part, one_hot_rows(dest_ref[pl.ds(g, 1), :]))
            totals[g] = moved[:8] + moved[8:16] + moved[16:24]
        return carry

    lax.fori_loop(0, ghosts // 4, squeeze, 0)
    fields = []
    for k, x in enumerate(own + [pool_ref[3, :own_tiles], pool_ref[4, :own_tiles]]):
        packed_ref[k, :own_tiles] = x
        packed_ref[k, own_tiles:] = totals[:ghosts, k, :]
        fields.append(packed_ref[k])
    norm = sum(c * c for c in fields[:3])
    ones = jnp.ones_like(norm)
    rows = []
    for c in fields[:3] + [norm]:
        rows += source_terms(c)
    rows += [ones, ones, ones] + list(three(0.5 * fields[4])) + list(three(fields[3])[:2])
    put_rows(stage, rows, FEATS, tiles)

    def turn(g, carry):
        for v in range(2):
            at = g * 2 + v
            cols = jnp.transpose(stage[pl.ds(at * LANES, LANES), :]).astype(jnp.bfloat16)
            for u in range(LANES // FEATS):
                far[at * (LANES // FEATS) + u] = cols[:, u * FEATS:(u + 1) * FEATS]
        return carry

    lax.fori_loop(0, tiles * FEATS // LANES // 2, turn, 0)
    radius = fields[4][:own_tiles]
    target_rows(own, 1.0 / (radius * radius), stage, near, own_tiles)
    spread_column(far, 30, 32, mass_b)
    totals[...] = jnp.zeros_like(totals)

    def add(first, height):
        def body(target, source, place, weight):
            sq = jnp.dot(far[source, first:first + height], near[target],
                         preferred_element_type=jnp.float32)
            sq = jnp.maximum(sq, TINY)
            ratio = sq * lax.rsqrt(sq)
            falloff = jnp.maximum(1.0 - ratio, 0.0)
            falloff = falloff * falloff
            term = falloff * falloff * ((ratio + 0.25) * mass_b[source, first:first + height])
            totals[place] += weight * jnp.sum(term.reshape(height // 8, 8, LANES), axis=0)
        return body

    half = LANES // 2
    sweep(own_ref, sizes_ref[0], times_ref, tiles, own_tiles, 8, add(0, LANES))
    sweep(ghost_ref, sizes_ref[1], times_ref, tiles, own_tiles, 16, add(0, half))

    @pl.when(more > 0)
    def _():
        sweep(ghost_ref, sizes_ref[1], times_ref, tiles, own_tiles, 4, add(half, half))

    summed = jnp.sum(totals[:own_tiles], axis=1)
    norm = KERNEL_NORM / (radius * radius * radius)
    density = norm * (4.0 * summed + pool_ref[3, :own_tiles])
    dens_ref[...] = density
    press_ref[...] = GAMMA_LESS * pool_ref[5, :own_tiles] / density


def accel_kernel(sizes_ref, own_ref, ghost_ref, times_ref, more_ref, far, packed_ref, dest_ref,
                 press_ref, press_far_ref, out_ref, stage, near, half_a, half_b, press_all, left, left_half,
                 totals):
    own_tiles = out_ref.shape[1]
    tiles = packed_ref.shape[1]
    ghosts = tiles - own_tiles
    half = LANES // 2
    zero = jnp.zeros((ghosts, LANES), jnp.float32)
    put_rows(stage, list(three(press_far_ref[...])) + [zero] * 13, 16, ghosts)

    def squeeze(block, carry):
        for u in range(4):
            g = block * 4 + u
            part = stage[pl.ds(g * 16, 16), :].astype(jnp.bfloat16)
            moved = by_last(part, one_hot_rows(dest_ref[pl.ds(g, 1), :]))
            press_all[pl.ds(own_tiles + g, 1), :] = moved[0:1] + moved[1:2] + moved[2:3]
        return carry

    lax.fori_loop(0, ghosts // 4, squeeze, 0)
    press_all[:own_tiles] = press_ref[...]
    own = [packed_ref[k, :own_tiles] for k in range(3)]
    target_rows(own, jnp.ones_like(own[0]), stage, near, own_tiles)
    spread_column(far, 27, 30, half_b)
    half_a[...] = 0.5 * packed_ref[4, :own_tiles]
    mass = packed_ref[3]
    load = mass * press_all[...]
    coords = [packed_ref[k] for k in range(3)]
    rows = [mass] + [mass * c for c in coords] + [load] + [load * c for c in coords]
    split = [three(row) for row in rows]
    put_rows(stage, [s[0] for s in split] + [s[1] for s in split], 16, tiles)

    def pack(block, carry):
        for u in range(4):
            t = block * 4 + u
            part = stage[pl.ds(t * 16, 16), :].astype(jnp.bfloat16)
            left[t] = jnp.concatenate([part, part], axis=1)
        return carry

    def pack_half(block, carry):
        for u in range(4):
            t = block * 4 + u
            part = stage[pl.ds((t + own_tiles) * 16, 16), :].astype(jnp.bfloat16)
            for v in range(2):
                piece = part[:, v * half:(v + 1) * half]
                left_half[v, t] = jnp.concatenate([piece, piece], axis=1)
        return carry

    lax.fori_loop(0, own_tiles // 4, pack, 0)
    lax.fori_loop(0, ghosts // 4, pack_half, 0)
    totals[...] = jnp.zeros_like(totals)

    def add(first, height, lhs):
        def body(target, source, place, weight):
            sq = jnp.dot(far[source, first:first + height], near[target],
                         preferred_element_type=jnp.float32)
            sq = jnp.maximum(sq, TINY)
            radius = half_b[source, first:first + height] + half_a[pl.ds(target, 1), :]
            dist = sq * lax.rsqrt(sq)
            guess = pl.reciprocal(radius, approx=True)
            inv = guess * (2.0 - radius * guess)
            fall = inv * jnp.maximum(1.0 - dist * inv, 0.0)
            wide = fall * inv
            slope = wide * wide * fall
            high = slope.astype(jnp.bfloat16)
            low = (slope - high.astype(jnp.float32)).astype(jnp.bfloat16)
            terms = jnp.concatenate([high, low], axis=0)
            totals[place] += weight * jnp.dot(lhs(source), terms, preferred_element_type=jnp.float32)
        return body

    sweep(own_ref, sizes_ref[0], times_ref, tiles, own_tiles, 8, add(0, LANES, lambda s: left[s]))
    sweep(ghost_ref, sizes_ref[1], times_ref, tiles, own_tiles, 16,
          add(0, half, lambda s: left_half[0, jnp.maximum(s - own_tiles, 0)]))

    @pl.when(more_ref[0] > 0)
    def _():
        sweep(ghost_ref, sizes_ref[1], times_ref, tiles, own_tiles, 4,
              add(half, half, lambda s: left_half[1, jnp.maximum(s - own_tiles, 0)]))

    folded = totals[:own_tiles, :8] + totals[:own_tiles, 8:]
    mixed = [press_ref[...] * folded[:, k] + folded[:, k + 4] for k in range(4)]
    for k in range(3):
        out_ref[k] = 20.0 * KERNEL_NORM * (own[k] * mixed[0] - mixed[k + 1])


SMEM = pl.BlockSpec(memory_space=pltpu.SMEM)
VMEM = pl.BlockSpec(memory_space=pltpu.VMEM)


def plan_call(count, pairs, own_tiles, tiles):
    slots = pairs.shape[1]
    shapes = [(2,), (slots + 1,), (slots + 1,), (own_tiles * tiles + LANES,)]
    return pl.pallas_call(
        functools.partial(plan_kernel, own_tiles=own_tiles, tiles=tiles),
        out_shape=[jax.ShapeDtypeStruct(shape, jnp.int32) for shape in shapes],
        in_specs=[SMEM, SMEM],
        out_specs=[SMEM] * 4,
        cost_estimate=pl.CostEstimate(flops=10 ** 7, bytes_accessed=10 ** 7, transcendentals=0),
        name="plan",
    )(count, pairs)


def density_call(plan, pool, own_tiles):
    tiles = pool.shape[1]
    flat = jax.ShapeDtypeStruct((own_tiles, LANES), jnp.float32)
    return pl.pallas_call(
        density_kernel,
        out_shape=(
            flat,
            flat,
            jax.ShapeDtypeStruct((tiles, LANES, FEATS), jnp.bfloat16),
            jax.ShapeDtypeStruct((5, tiles, LANES), jnp.float32),
            jax.ShapeDtypeStruct((tiles - own_tiles, LANES), jnp.int32),
            jax.ShapeDtypeStruct((1,), jnp.int32),
        ),
        in_specs=[SMEM] * 4 + [VMEM],
        out_specs=(VMEM, VMEM, VMEM, VMEM, VMEM, SMEM),
        scratch_shapes=[
            pltpu.VMEM((tiles * FEATS, LANES), jnp.float32),
            pltpu.VMEM((own_tiles, FEATS, LANES), jnp.bfloat16),
            pltpu.VMEM((tiles, LANES, LANES), jnp.float32),
            pltpu.VMEM((max(own_tiles, tiles - own_tiles) + 1, 8, LANES), jnp.float32),
        ],
        name="density",
    )(*plan, pool)


def accel_call(plan, more, far, packed, dest, press, press_far):
    own_tiles = press.shape[0]
    tiles = packed.shape[1]
    return pl.pallas_call(
        accel_kernel,
        out_shape=jax.ShapeDtypeStruct((3, own_tiles, LANES), jnp.float32),
        in_specs=[SMEM] * 5 + [VMEM] * 5,
        out_specs=VMEM,
        scratch_shapes=[
            pltpu.VMEM((tiles * FEATS, LANES), jnp.float32),
            pltpu.VMEM((own_tiles, FEATS, LANES), jnp.bfloat16),
            pltpu.VMEM((own_tiles, LANES), jnp.float32),
            pltpu.VMEM((tiles, LANES, LANES), jnp.float32),
            pltpu.VMEM((tiles, LANES), jnp.float32),
            pltpu.VMEM((own_tiles, 16, 2 * LANES), jnp.bfloat16),
            pltpu.VMEM((2, tiles - own_tiles, 16, LANES), jnp.bfloat16),
            pltpu.VMEM((own_tiles + 1, 16, LANES), jnp.float32),
        ],
        name="accel",
    )(*plan, more, far, packed, dest, press, press_far)


def local(positions, mass, smoothing, energy, destination, pairs, pair_count):
    across = lax.axis_size("gx")
    beside = lax.axis_size("gy")
    domains = across * beside
    dev_rows = mass.shape[0]
    slot_count = dev_rows // domains
    own_tiles = dev_rows // LANES
    edge_rows = GT * LANES
    plan = plan_call(pair_count, pairs, own_tiles, own_tiles + 4 * GT)
    fields = jnp.concatenate([positions, mass[None], smoothing[None], energy[None]], 0)
    ordered = lax.sort(
        (destination[:, 0],) + tuple(fields[k] for k in range(6)), num_keys=1, is_stable=True
    )
    outgoing = jnp.stack([row.reshape(domains, slot_count) for row in ordered[1:]], 1)
    outgoing = outgoing.reshape(across, beside, 6 * slot_count)
    halfway = lax.all_to_all(outgoing, "gy", split_axis=1, concat_axis=1, tiled=True)
    moved = lax.all_to_all(halfway, "gx", split_axis=0, concat_axis=0, tiled=True)
    settled = jnp.transpose(moved.reshape(domains, 6, slot_count), (1, 0, 2)).reshape(6, dev_rows)
    boundary = settled[:, :edge_rows].reshape(6, 1, 1, edge_rows)
    ghosts = extended(boundary, (("gx", 1), ("gy", 2)), 1)
    extra = neighbour_rows(ghosts)
    pool = jnp.concatenate([settled, extra], 1).reshape(6, own_tiles + 4 * GT, LANES)
    density, press, far, packed, dest, more = density_call(plan, pool, own_tiles)
    press_edge = press.reshape(-1)[:edge_rows].reshape(1, 1, edge_rows)
    press_ghosts = extended(press_edge, (("gx", 0), ("gy", 1)), 1)
    press_far = neighbour_rows(press_ghosts).reshape(4 * GT, LANES)
    accel = accel_call(plan, more, far, packed, dest, press, press_far)
    return (density.reshape(-1), accel.reshape(3, -1))


def solution(mesh):
    placed = (
        P(None, ("gx", "gy")),
        P(("gx", "gy")),
        P(("gx", "gy")),
        P(("gx", "gy")),
        P(("gx", "gy"), None),
        P(None, ("gx", "gy")),
        P(("gx", "gy")),
    )
    return jax.shard_map(
        local,
        mesh=mesh,
        in_specs=placed,
        out_specs=(P(("gx", "gy")), P(None, ("gx", "gy"))),
        check_vma=False,
    )
```

```python
import functools
import math

import jax
import jax.numpy as jnp
from jax import lax
from jax.experimental import pallas as pl
from jax.experimental.pallas import tpu as pltpu
from jax.sharding import PartitionSpec as P

GT = 8
LANES = 128
FEATS = 32
TINY = 1e-12

KERNEL_NORM = 21.0 / (2.0 * math.pi)
GAMMA_LESS = 2.0 / 3.0


def extended(block, sides, width):
    for axis, dim in sides:
        count = lax.axis_size(axis)
        forward = [(i, i + 1) for i in range(count - 1)]
        backward = [(target, source) for source, target in forward]
        low = lax.ppermute(
            lax.slice_in_dim(block, block.shape[dim] - width, None, axis=dim), axis, forward
        )
        high = lax.ppermute(lax.slice_in_dim(block, 0, width, axis=dim), axis, backward)
        block = jnp.concatenate([low, block, high], axis=dim)
    return block


def neighbour_rows(ghosts):
    return jnp.concatenate(
        [ghosts[..., 0, 1, :], ghosts[..., 2, 1, :], ghosts[..., 1, 0, :], ghosts[..., 1, 2, :]],
        axis=-1,
    )


def three(x):
    one = x.astype(jnp.bfloat16).astype(jnp.float32)
    rest = x - one
    two = rest.astype(jnp.bfloat16).astype(jnp.float32)
    return one, two, (rest - two).astype(jnp.bfloat16).astype(jnp.float32)


def source_terms(x):
    one, two, low = three(x)
    return [one, two, one, two, low, one]


def target_terms(x):
    one, two, low = three(x)
    return [one, one, two, two, one, low]


def put_rows(stage, rows, width, tiles):
    for k, row in enumerate(rows):
        stage[pl.ds(k, tiles, stride=width), :] = row


def plan_kernel(count_ref, pairs_ref, sizes_ref, own_ref, ghost_ref, times_ref, own_tiles, tiles):
    step = 16

    def clear(block, carry):
        for u in range(step):
            times_ref[block * step + u] = 0
        return carry

    lax.fori_loop(0, times_ref.shape[0] // step, clear, 0)

    count = count_ref[0]
    spare = own_tiles * tiles
    last = pairs_ref.shape[1] - 1
    ahead = 8

    def add(block, carry):
        own, ghost = carry
        picked = []
        for u in range(ahead):
            k = block * ahead + u
            live = k < count
            at = jnp.minimum(k, last)
            source = jnp.where(live, pairs_ref[1, at], 0)
            key = jnp.where(live, pairs_ref[0, at] * tiles + source, spare)
            near = (source < own_tiles).astype(jnp.int32)
            alive = live.astype(jnp.int32)
            picked.append((key, near * alive, (1 - near) * alive))
        for key, near, beyond in picked:
            seen = times_ref[key]
            times_ref[key] = seen + 1
            own_ref[own] = key
            ghost_ref[ghost] = key
            fresh = (seen == 0).astype(jnp.int32)
            own = own + fresh * near
            ghost = ghost + fresh * beyond
        return own, ghost

    own, ghost = lax.fori_loop(0, (count + ahead - 1) // ahead, add, (0, 0))
    sizes_ref[0] = own
    sizes_ref[1] = ghost


def one_hot_rows(dest):
    rows = lax.broadcasted_iota(jnp.int32, (LANES, LANES), 0)
    wide = jnp.broadcast_to(dest, (LANES, LANES))
    return jnp.where(wide == rows, 1.0, 0.0).astype(jnp.bfloat16)


def by_last(a, b):
    return lax.dot_general(a, b, (((1,), (1,)), ((), ())), preferred_element_type=jnp.float32)


def sweep(list_ref, size, times_ref, tiles, dump, unroll, body):
    last = list_ref.shape[0] - 1

    def advance(block, carry):
        for u in range(unroll):
            k = block * unroll + u
            live = k < size
            key = jnp.where(live, list_ref[jnp.minimum(k, last)], 0)
            target = key // tiles
            source = key - target * tiles
            weight = times_ref[key].astype(jnp.float32)
            body(target, source, jnp.where(live, target, dump), weight)
        return carry

    lax.fori_loop(0, (size + unroll - 1) // unroll, advance, 0)


def keep_rows(stage, near, tiles):
    group = 4

    def keep(block, carry):
        for u in range(group):
            t = block * group + u
            near[t] = stage[pl.ds(t * FEATS, FEATS), :].astype(jnp.bfloat16)
        return carry

    lax.fori_loop(0, tiles // group, keep, 0)


def target_rows(coords, scale, stage, near, tiles):
    norm = sum(c * c for c in coords)
    zero = jnp.zeros_like(norm)
    rows = []
    for c in coords:
        rows += target_terms(-2.0 * c * scale)
    rows += target_terms(scale)
    rows += list(three(norm * scale))
    rows += [zero] * (FEATS - len(rows))
    put_rows(stage, rows, FEATS, tiles)
    keep_rows(stage, near, tiles)


def spread_column(far, first, last, wide):
    row = lax.broadcasted_iota(jnp.int32, (FEATS, LANES), 0)
    pick = jnp.where((row >= first) & (row < last), 1.0, 0.0).astype(jnp.bfloat16)
    group = 4

    def one(block, carry):
        for u in range(group):
            t = block * group + u
            wide[t] = jnp.dot(far[t], pick, preferred_element_type=jnp.float32)
        return carry

    lax.fori_loop(0, wide.shape[0] // group, one, 0)


def density_kernel(sizes_ref, own_ref, ghost_ref, times_ref, pool_ref,
                   dens_ref, press_ref, far, packed_ref, dest_ref, more_ref,
                   stage, near, mass_b, totals):
    own_tiles = dens_ref.shape[0]
    tiles = pool_ref.shape[1]
    ghosts = tiles - own_tiles
    own, out_of_reach = [], 0.0
    ghost = []
    reach = jnp.max(pool_ref[4]) + 0.01
    for k in range(3):
        x = pool_ref[k, :own_tiles]
        low, high = jnp.min(x), jnp.max(x)
        centre = 0.5 * (low + high)
        far_x = pool_ref[k, own_tiles:]
        gap = jnp.maximum(jnp.maximum(low - far_x, far_x - high), 0.0)
        out_of_reach = out_of_reach + gap * gap
        own.append(x - centre)
        ghost.append(far_x - centre)
    ghost_mass = pool_ref[3, own_tiles:]
    active = (out_of_reach < reach * reach) & (ghost_mass != 0.0)
    upto = lax.broadcasted_iota(jnp.int32, (LANES, LANES), 0) <= lax.broadcasted_iota(
        jnp.int32, (LANES, LANES), 1)
    upto = jnp.where(upto, 1.0, 0.0).astype(jnp.bfloat16)
    flags = jnp.where(active, 1.0, 0.0).astype(jnp.bfloat16)
    rank = jnp.dot(flags, upto, preferred_element_type=jnp.float32)
    dest = jnp.where(active, rank - 1.0, -1.0).astype(jnp.int32)
    dest_ref[...] = dest
    most = jnp.max(rank)
    more = (most > LANES // 2 + 0.5).astype(jnp.int32)
    more_ref[0] = more
    split = [three(x) for x in ghost + [ghost_mass, pool_ref[4, own_tiles:]]]
    zero = jnp.zeros_like(ghost_mass)
    rows = []
    for term in range(3):
        rows += [s[term] for s in split] + [zero] * 3
    put_rows(stage, rows + [zero] * 8, FEATS, ghosts)

    def squeeze(block, carry):
        for u in range(4):
            g = block * 4 + u
            part = stage[pl.ds(g * FEATS, FEATS), :].astype(jnp.bfloat16)
            moved = by_last(part, one_hot_rows(dest_ref[pl.ds(g, 1), :]))
            totals[g] = moved[:8] + moved[8:16] + moved[16:24]
        return carry

    lax.fori_loop(0, ghosts // 4, squeeze, 0)
    fields = []
    for k, x in enumerate(own + [pool_ref[3, :own_tiles], pool_ref[4, :own_tiles]]):
        packed_ref[k, :own_tiles] = x
        packed_ref[k, own_tiles:] = totals[:ghosts, k, :]
        fields.append(packed_ref[k])
    norm = sum(c * c for c in fields[:3])
    ones = jnp.ones_like(norm)
    rows = []
    for c in fields[:3] + [norm]:
        rows += source_terms(c)
    rows += [ones, ones, ones] + list(three(0.5 * fields[4])) + list(three(fields[3])[:2])
    put_rows(stage, rows, FEATS, tiles)

    def turn(g, carry):
        for v in range(2):
            at = g * 2 + v
            cols = jnp.transpose(stage[pl.ds(at * LANES, LANES), :]).astype(jnp.bfloat16)
            for u in range(LANES // FEATS):
                far[at * (LANES // FEATS) + u] = cols[:, u * FEATS:(u + 1) * FEATS]
        return carry

    lax.fori_loop(0, tiles * FEATS // LANES // 2, turn, 0)
    radius = fields[4][:own_tiles]
    target_rows(own, 1.0 / (radius * radius), stage, near, own_tiles)
    spread_column(far, 30, 32, mass_b)
    totals[...] = jnp.zeros_like(totals)

    def add(first, height):
        def body(target, source, place, weight):
            sq = jnp.dot(far[source, first:first + height], near[target],
                         preferred_element_type=jnp.float32)
            sq = jnp.maximum(sq, TINY)
            ratio = sq * lax.rsqrt(sq)
            falloff = jnp.maximum(1.0 - ratio, 0.0)
            falloff = falloff * falloff
            term = falloff * falloff * ((ratio + 0.25) * mass_b[source, first:first + height])
            totals[place] += weight * jnp.sum(term.reshape(height // 8, 8, LANES), axis=0)
        return body

    half = LANES // 2
    sweep(own_ref, sizes_ref[0], times_ref, tiles, own_tiles, 16, add(0, LANES))
    sweep(ghost_ref, sizes_ref[1], times_ref, tiles, own_tiles, 32, add(0, half))

    @pl.when(more > 0)
    def _():
        sweep(ghost_ref, sizes_ref[1], times_ref, tiles, own_tiles, 4, add(half, half))

    summed = jnp.sum(totals[:own_tiles], axis=1)
    norm = KERNEL_NORM / (radius * radius * radius)
    density = norm * (4.0 * summed + pool_ref[3, :own_tiles])
    dens_ref[...] = density
    press_ref[...] = GAMMA_LESS * pool_ref[5, :own_tiles] / density


def accel_kernel(sizes_ref, own_ref, ghost_ref, times_ref, more_ref, far, packed_ref, dest_ref,
                 press_ref, press_far_ref, out_ref, stage, near, half_a, half_b, press_all, left, left_half,
                 totals):
    own_tiles = out_ref.shape[1]
    tiles = packed_ref.shape[1]
    ghosts = tiles - own_tiles
    half = LANES // 2
    zero = jnp.zeros((ghosts, LANES), jnp.float32)
    put_rows(stage, list(three(press_far_ref[...])) + [zero] * 13, 16, ghosts)

    def squeeze(block, carry):
        for u in range(4):
            g = block * 4 + u
            part = stage[pl.ds(g * 16, 16), :].astype(jnp.bfloat16)
            moved = by_last(part, one_hot_rows(dest_ref[pl.ds(g, 1), :]))
            press_all[pl.ds(own_tiles + g, 1), :] = moved[0:1] + moved[1:2] + moved[2:3]
        return carry

    lax.fori_loop(0, ghosts // 4, squeeze, 0)
    press_all[:own_tiles] = press_ref[...]
    own = [packed_ref[k, :own_tiles] for k in range(3)]
    target_rows(own, jnp.ones_like(own[0]), stage, near, own_tiles)
    spread_column(far, 27, 30, half_b)
    half_a[...] = 0.5 * packed_ref[4, :own_tiles]
    mass = packed_ref[3]
    load = mass * press_all[...]
    coords = [packed_ref[k] for k in range(3)]
    rows = [mass] + [mass * c for c in coords] + [load] + [load * c for c in coords]
    split = [three(row) for row in rows]
    put_rows(stage, [s[0] for s in split] + [s[1] for s in split], 16, tiles)

    def pack(block, carry):
        for u in range(4):
            t = block * 4 + u
            part = stage[pl.ds(t * 16, 16), :].astype(jnp.bfloat16)
            left[t] = jnp.concatenate([part, part], axis=1)
        return carry

    def pack_half(block, carry):
        for u in range(4):
            t = block * 4 + u
            part = stage[pl.ds((t + own_tiles) * 16, 16), :].astype(jnp.bfloat16)
            for v in range(2):
                piece = part[:, v * half:(v + 1) * half]
                left_half[v, t] = jnp.concatenate([piece, piece], axis=1)
        return carry

    lax.fori_loop(0, own_tiles // 4, pack, 0)
    lax.fori_loop(0, ghosts // 4, pack_half, 0)
    totals[...] = jnp.zeros_like(totals)

    def add(first, height, lhs):
        def body(target, source, place, weight):
            sq = jnp.dot(far[source, first:first + height], near[target],
                         preferred_element_type=jnp.float32)
            sq = jnp.maximum(sq, TINY)
            radius = half_b[source, first:first + height] + half_a[pl.ds(target, 1), :]
            dist = sq * lax.rsqrt(sq)
            guess = pl.reciprocal(radius, approx=True)
            inv = guess * (2.0 - radius * guess)
            fall = inv * jnp.maximum(1.0 - dist * inv, 0.0)
            wide = fall * inv
            slope = wide * wide * fall
            high = slope.astype(jnp.bfloat16)
            low = (slope - high.astype(jnp.float32)).astype(jnp.bfloat16)
            terms = jnp.concatenate([high, low], axis=0)
            totals[place] += weight * jnp.dot(lhs(source), terms, preferred_element_type=jnp.float32)
        return body

    sweep(own_ref, sizes_ref[0], times_ref, tiles, own_tiles, 16, add(0, LANES, lambda s: left[s]))
    sweep(ghost_ref, sizes_ref[1], times_ref, tiles, own_tiles, 32,
          add(0, half, lambda s: left_half[0, jnp.maximum(s - own_tiles, 0)]))

    @pl.when(more_ref[0] > 0)
    def _():
        sweep(ghost_ref, sizes_ref[1], times_ref, tiles, own_tiles, 4,
              add(half, half, lambda s: left_half[1, jnp.maximum(s - own_tiles, 0)]))

    folded = totals[:own_tiles, :8] + totals[:own_tiles, 8:]
    mixed = [press_ref[...] * folded[:, k] + folded[:, k + 4] for k in range(4)]
    for k in range(3):
        out_ref[k] = 20.0 * KERNEL_NORM * (own[k] * mixed[0] - mixed[k + 1])


SMEM = pl.BlockSpec(memory_space=pltpu.SMEM)
VMEM = pl.BlockSpec(memory_space=pltpu.VMEM)


def plan_call(count, pairs, own_tiles, tiles):
    slots = pairs.shape[1]
    shapes = [(2,), (slots + 1,), (slots + 1,), (own_tiles * tiles + LANES,)]
    return pl.pallas_call(
        functools.partial(plan_kernel, own_tiles=own_tiles, tiles=tiles),
        out_shape=[jax.ShapeDtypeStruct(shape, jnp.int32) for shape in shapes],
        in_specs=[SMEM, SMEM],
        out_specs=[SMEM] * 4,
        cost_estimate=pl.CostEstimate(flops=10 ** 7, bytes_accessed=10 ** 7, transcendentals=0),
        name="plan",
    )(count, pairs)


def density_call(plan, pool, own_tiles):
    tiles = pool.shape[1]
    flat = jax.ShapeDtypeStruct((own_tiles, LANES), jnp.float32)
    return pl.pallas_call(
        density_kernel,
        out_shape=(
            flat,
            flat,
            jax.ShapeDtypeStruct((tiles, LANES, FEATS), jnp.bfloat16),
            jax.ShapeDtypeStruct((5, tiles, LANES), jnp.float32),
            jax.ShapeDtypeStruct((tiles - own_tiles, LANES), jnp.int32),
            jax.ShapeDtypeStruct((1,), jnp.int32),
        ),
        in_specs=[SMEM] * 4 + [VMEM],
        out_specs=(VMEM, VMEM, VMEM, VMEM, VMEM, SMEM),
        scratch_shapes=[
            pltpu.VMEM((tiles * FEATS, LANES), jnp.float32),
            pltpu.VMEM((own_tiles, FEATS, LANES), jnp.bfloat16),
            pltpu.VMEM((tiles, LANES, LANES), jnp.float32),
            pltpu.VMEM((max(own_tiles, tiles - own_tiles) + 1, 8, LANES), jnp.float32),
        ],
        name="density",
    )(*plan, pool)


def accel_call(plan, more, far, packed, dest, press, press_far):
    own_tiles = press.shape[0]
    tiles = packed.shape[1]
    return pl.pallas_call(
        accel_kernel,
        out_shape=jax.ShapeDtypeStruct((3, own_tiles, LANES), jnp.float32),
        in_specs=[SMEM] * 5 + [VMEM] * 5,
        out_specs=VMEM,
        scratch_shapes=[
            pltpu.VMEM((tiles * FEATS, LANES), jnp.float32),
            pltpu.VMEM((own_tiles, FEATS, LANES), jnp.bfloat16),
            pltpu.VMEM((own_tiles, LANES), jnp.float32),
            pltpu.VMEM((tiles, LANES, LANES), jnp.float32),
            pltpu.VMEM((tiles, LANES), jnp.float32),
            pltpu.VMEM((own_tiles, 16, 2 * LANES), jnp.bfloat16),
            pltpu.VMEM((2, tiles - own_tiles, 16, LANES), jnp.bfloat16),
            pltpu.VMEM((own_tiles + 1, 16, LANES), jnp.float32),
        ],
        name="accel",
    )(*plan, more, far, packed, dest, press, press_far)


def local(positions, mass, smoothing, energy, destination, pairs, pair_count):
    across = lax.axis_size("gx")
    beside = lax.axis_size("gy")
    domains = across * beside
    dev_rows = mass.shape[0]
    slot_count = dev_rows // domains
    own_tiles = dev_rows // LANES
    edge_rows = GT * LANES
    plan = plan_call(pair_count, pairs, own_tiles, own_tiles + 4 * GT)
    fields = jnp.concatenate([positions, mass[None], smoothing[None], energy[None]], 0)
    ordered = lax.sort(
        (destination[:, 0],) + tuple(fields[k] for k in range(6)), num_keys=1, is_stable=True
    )
    outgoing = jnp.stack([row.reshape(domains, slot_count) for row in ordered[1:]], 1)
    outgoing = outgoing.reshape(across, beside, 6 * slot_count)
    halfway = lax.all_to_all(outgoing, "gy", split_axis=1, concat_axis=1, tiled=True)
    moved = lax.all_to_all(halfway, "gx", split_axis=0, concat_axis=0, tiled=True)
    settled = jnp.transpose(moved.reshape(domains, 6, slot_count), (1, 0, 2)).reshape(6, dev_rows)
    boundary = settled[:, :edge_rows].reshape(6, 1, 1, edge_rows)
    ghosts = extended(boundary, (("gx", 1), ("gy", 2)), 1)
    extra = neighbour_rows(ghosts)
    pool = jnp.concatenate([settled, extra], 1).reshape(6, own_tiles + 4 * GT, LANES)
    density, press, far, packed, dest, more = density_call(plan, pool, own_tiles)
    press_edge = press.reshape(-1)[:edge_rows].reshape(1, 1, edge_rows)
    press_ghosts = extended(press_edge, (("gx", 0), ("gy", 1)), 1)
    press_far = neighbour_rows(press_ghosts).reshape(4 * GT, LANES)
    accel = accel_call(plan, more, far, packed, dest, press, press_far)
    return (density.reshape(-1), accel.reshape(3, -1))


def solution(mesh):
    placed = (
        P(None, ("gx", "gy")),
        P(("gx", "gy")),
        P(("gx", "gy")),
        P(("gx", "gy")),
        P(("gx", "gy"), None),
        P(None, ("gx", "gy")),
        P(("gx", "gy")),
    )
    return jax.shard_map(
        local,
        mesh=mesh,
        in_specs=placed,
        out_specs=(P(("gx", "gy")), P(None, ("gx", "gy"))),
        check_vma=False,
    )
```
